128 devices in a mesh: gx: 8 (over y_hi, z), gy: 16 (over y_lo, x, core).
Axes of the slice: x: 4, y: 4 (y_hi: 2, y_lo: 2; y = y_hi * 2 + y_lo), z: 4, core: 2. Of those that a mesh axis runs over, the one named last changes fastest.
Arguments:
- basis3: float32 [262144, 256], P(('gx', 'gy')), may hold values from -0.046875 to 0.046875
- basis2: float32 [262144, 256], P(('gx', 'gy')), may hold values from -0.03125 to 0.03125
- basis1: float32 [262144, 256], P(('gx', 'gy')), may hold values from -0.0234375 to 0.0234375
- leaf_inverse: float32 [262144], P(('gx', 'gy')), may hold values from 0.25 to 4
- rhs: float32 [262144, 256], P(('gx', 'gy')), may hold values from -6 to 6
- coupling3: float32 [4, 512, 512], replicated, may hold values from -1.5 to 1.5
- coupling2: float32 [2, 512, 512], replicated, may hold values from -1.5 to 1.5
- coupling1: float32 [1, 512, 512], replicated, may hold values from -1.5 to 1.5
Outputs:
- solution: float32 [262144, 256], P(('gx', 'gy'))
- core3: float32 [2048, 512], P(('gx', 'gy'))
- core2: float32 [1024, 512], P(('gx', 'gy'))
- core1: float32 [512, 512], P(('gx', 'gy'))
The draws below stay inside these ranges and needn't reach their ends.
All inputs are finite; a program needn't handle non-finite values.
Results may differ from the reference program's by a relative error of at most 0.0003.
Values sent between devices are 32-bit elements; how exact they have to be, the bound alone decides.
A program may use at most 128 MiB of HBM per device.

```python
import math
import jax
import jax.numpy as jnp
from jax import lax

R = 256
NRHS = 256
N = 262144


def shard_levels(own_key, dims, pieces, least, high):
    loudness = 1.0
    for axis_at, blocks in pieces:
        draws = jax.random.uniform(jax.random.fold_in(jax.random.fold_in(own_key, 6), axis_at), (blocks,), jnp.float32, least / len(pieces), high / len(pieces))
        loudness = loudness * jnp.repeat(jnp.exp(draws), dims[axis_at] // blocks).reshape((-1,) + (1,) * (len(dims) - 1 - axis_at))
    return loudness


def noise(stream_key, extent, spread, most, split=(), held_as=jnp.bfloat16):
    factor_of = shard_levels(stream_key, extent, split, -0.22, 0.18) if split else 1.0
    drawn = jax.random.normal(stream_key, extent, jnp.float32) * spread * factor_of
    return jnp.minimum(jnp.maximum(drawn, -most), most).astype(held_as)


def setup_inputs(seed: int = 0) -> dict:
    splits = jax.random.split(jax.random.key(seed), 9)
    return {
        "basis3": noise(splits[0], (N, R), (N // 16) ** -0.5, 0.046875, ((0, 128),), jnp.float32),
        "basis2": noise(splits[1], (N, R), (N // 8) ** -0.5, 0.03125, ((0, 128),), jnp.float32),
        "basis1": noise(splits[2], (N, R), (N // 4) ** -0.5, 0.0234375, ((0, 128),), jnp.float32),
        "leaf_inverse": jnp.clip(jnp.exp(math.log(4.0) - 2.7725887 * jax.random.uniform(splits[3], (N,), jnp.float32) ** shard_levels(splits[3], (N,), ((0, 128),), -0.2, 0.2)), 0.25, 4.0),
        "rhs": noise(splits[4], (N, NRHS), 1.0, 6.0, ((0, 128),), jnp.float32),
        "coupling3": noise(splits[5], (4, 2 * R, 2 * R), (R // 16) ** -0.5, 1.5, (), jnp.float32),
        "coupling2": noise(splits[6], (2, 2 * R, 2 * R), (R // 16) ** -0.5, 1.5, (), jnp.float32),
        "coupling1": noise(splits[7], (1, 2 * R, 2 * R), (R // 16) ** -0.5, 1.5, (), jnp.float32),
    }


highest_precision = lax.Precision.HIGHEST

def core_solve(coupling_full, gram_upper, gram_lower):
    basis_rank = gram_upper.shape[0]
    upper_rows = coupling_full[:basis_rank]
    lower_rows = coupling_full[basis_rank:]
    inner = jnp.dot(upper_rows.T.astype(jnp.float32), jnp.dot(gram_upper.astype(jnp.float32), upper_rows.astype(jnp.float32), precision=highest_precision, preferred_element_type=jnp.float32).astype(jnp.float32), precision=highest_precision, preferred_element_type=jnp.float32)
    inner = inner + jnp.dot(lower_rows.T.astype(jnp.float32), jnp.dot(gram_lower.astype(jnp.float32), lower_rows.astype(jnp.float32), precision=highest_precision, preferred_element_type=jnp.float32).astype(jnp.float32), precision=highest_precision, preferred_element_type=jnp.float32)
    inner = 0.5 * (inner + inner.T) + jnp.eye(2 * basis_rank, dtype=jnp.float32)
    factor = jnp.linalg.cholesky(inner)
    half_solve = lax.linalg.triangular_solve(factor, coupling_full.T, left_side=True, lower=True)
    return jnp.dot(half_solve.T.astype(jnp.float32), half_solve.astype(jnp.float32), precision=highest_precision, preferred_element_type=jnp.float32)

def reference(basis3, basis2, basis1, leaf_inverse, rhs, coupling3, coupling2, coupling1):
    solved = jnp.concatenate([basis3, basis2, basis1, rhs], axis=1) * leaf_inverse[:, None]
    basis_rank = basis3.shape[1]
    total_rows = basis3.shape[0]
    core_list = []
    for tree_level, basis_now, coupling_now in ((3, basis3, coupling3), (2, basis2, coupling2), (1, basis1, coupling1)):
        block_count = 2 ** tree_level
        block_rows = total_rows // block_count
        basis_blocks = basis_now.reshape(block_count, block_rows, basis_rank)
        solved_blocks = solved.reshape(block_count, block_rows, solved.shape[1])
        grams = jnp.einsum('cnr,cnw->crw', basis_blocks, solved_blocks, precision=highest_precision)
        updates = []
        level_cores = []
        for pair_index in range(block_count // 2):
            upper_gram = grams[2 * pair_index]
            lower_gram = grams[2 * pair_index + 1]
            core_full = core_solve(coupling_now[pair_index], upper_gram[:, :basis_rank], lower_gram[:, :basis_rank])
            stacked = jnp.concatenate([upper_gram[:, basis_rank:], lower_gram[:, basis_rank:]], axis=0)
            updates.append(jnp.dot(core_full[:basis_rank].astype(jnp.float32), stacked.astype(jnp.float32), precision=highest_precision, preferred_element_type=jnp.float32))
            updates.append(jnp.dot(core_full[basis_rank:].astype(jnp.float32), stacked.astype(jnp.float32), precision=highest_precision, preferred_element_type=jnp.float32))
            level_cores.append(core_full)
        update_blocks = jnp.stack(updates)
        reduced = solved_blocks[:, :, basis_rank:] - jnp.einsum('cnr,crw->cnw', solved_blocks[:, :, :basis_rank], update_blocks, precision=highest_precision)
        solved = reduced.reshape(total_rows, reduced.shape[2])
        core_list.append(jnp.concatenate(level_cores, axis=0))
    return (solved, core_list[0], core_list[1], core_list[2])
```

```python
import jax
import jax.numpy as jnp
from jax import lax
from jax.experimental import pallas as pl
from jax.experimental.pallas import tpu as pltpu
from jax.sharding import PartitionSpec as P

F32 = jnp.float32
BF16 = jnp.bfloat16
NN = ((1,), (0,))
TN = ((0,), (0,))
W = 16
NB = 128
VMEM = pl.BlockSpec(memory_space=pltpu.VMEM)


def dot6(a, b, dims):
    return lax.dot_general(
        a, b, (dims, ((), ())), precision=lax.Precision.HIGHEST, preferred_element_type=F32
    )


def dot1(a, b, dims):
    return lax.dot_general(a, b, (dims, ((), ())), preferred_element_type=F32)


def split2(x):
    hi = x.astype(BF16)
    return hi, (x - hi.astype(F32)).astype(BF16)


def split3(x):
    hi = x.astype(BF16)
    rest = x - hi.astype(F32)
    mid = rest.astype(BF16)
    return hi, mid, (rest - mid.astype(F32)).astype(BF16)


def dot3(a, b, dims):
    return dot1(a[0], b[0], dims) + (dot1(a[0], b[1], dims) + dot1(a[1], b[0], dims))


def gram_kernel(b3, b2, b1, rhs, leaf, first, rest):
    @pl.when(pl.program_id(0) == 0)
    def _():
        first[...] = jnp.zeros_like(first)
        rest[...] = jnp.zeros_like(rest)

    root = jnp.sqrt(leaf[...])
    t3, t2, t1, tr = (split2(x[...] * root) for x in (b3, b2, b1, rhs))
    r = b3.shape[1]
    first[...] += dot3(t3, t3, TN)
    at = 0
    for left, rights in ((t3, (t2, t1, tr)), (t2, (t2, t1, tr)), (t1, (t1, tr))):
        for right in rights:
            rest[:, at : at + r] += dot3(left, right, TN)
            at += r


def grams(b3, b2, b1, rhs, leaf):
    rows, r = b3.shape
    tile = 512
    block = pl.BlockSpec((tile, r), lambda i: (i, 0))
    return pl.pallas_call(
        gram_kernel,
        grid=(rows // tile,),
        in_specs=[block] * 4 + [pl.BlockSpec((tile, 1), lambda i: (i, 0))],
        out_specs=[pl.BlockSpec((r, r), lambda i: (0, 0)), pl.BlockSpec((r, 8 * r), lambda i: (0, 0))],
        out_shape=[jax.ShapeDtypeStruct((r, r), F32), jax.ShapeDtypeStruct((r, 8 * r), F32)],
        name="grams",
    )(b3, b2, b1, rhs, leaf[:, None])


def invert_factor(work, cols, rows, panel):
    n = work.shape[0]
    lane = lax.broadcasted_iota(jnp.int32, (W, n), 1)
    sub = lax.broadcasted_iota(jnp.int32, (W, n), 0)
    for s in range(n // W):
        o = s * W
        block = work[o : o + W, :]
        for k in range(W):
            cols[k * W : (k + 1) * W, :] = jnp.broadcast_to(block[:, o + k : o + k + 1], (W, n))
        inside = (lane >= o) & (lane < o + W)
        rows[...] = jnp.where(inside, jnp.where(lane - o == sub, 1.0, 0.0), block)
        c = {(i, k): cols[i * W + k : i * W + k + 1, :] for i in range(W) for k in range(i + 1)}
        x = [rows[i : i + 1, :] for i in range(W)]
        for k in range(W):
            recip = 1.0 / c[k, k]
            for i in range(k + 1, W):
                m = c[i, k] * recip
                for j in range(k + 1, i + 1):
                    c[i, j] = c[i, j] - m * c[j, k]
                x[i] = x[i] - m * x[k]
            panel[k : k + 1, :] = x[k] * lax.rsqrt(c[k, k])
        v = panel[...]
        work[o : o + W, :] = jnp.where(lane < o + W, v, 0.0)
        t = o + W
        if t < n:
            v1, v2, v3 = split3(v)
            left = jnp.concatenate([v1, v1, v2, v1, v3, v2], 0)
            right = jnp.concatenate([v1, v2, v1, v3, v1, v2], 0)
            update = dot1(left, right, TN)
            below = lax.broadcasted_iota(jnp.int32, (n - t, n), 1)
            kept = jnp.where((below >= o) & (below < t), 0.0, work[t:, :])
            work[t:, :] = kept - update[t:, :]


def factor_kernel(g, coupling, m, c, work, cols, rows, panel):
    r = g.shape[1]
    order = 2 * r
    steps = order // NB
    gl = jnp.concatenate(
        [dot6(g[:r, :], coupling[:r, :], NN), dot6(g[r:, :], coupling[r:, :], NN)], 0
    )
    eye = jnp.where(
        lax.broadcasted_iota(jnp.int32, (NB, NB), 0) == lax.broadcasted_iota(jnp.int32, (NB, NB), 1),
        1.0,
        0.0,
    )
    full = coupling[...]
    for j in range(steps):
        o = j * NB
        c[o : o + NB, o:order] = dot6(full[:, o : o + NB], gl[:, o:], TN)
        c[o : o + NB, order:] = full[:, o : o + NB].T

    def step(j, carry):
        for jj in range(steps):

            @pl.when(j == jj)
            def _(o=jj * NB):
                work[...] = c[o : o + NB, o : o + NB] + eye

        invert_factor(work, cols, rows, panel)
        for jj in range(steps):

            @pl.when(j == jj)
            def _(jj=jj, o=jj * NB, t=jj * NB + NB):
                out = dot6(work[...], c[o : o + NB, t:], NN)
                m[o : o + NB, :] = out[:, order - t :]
                for q in range(jj + 1, steps):
                    w = q * NB
                    c[w : w + NB, w:] = c[w : w + NB, w:] - dot6(
                        out[:, w - t : w - t + NB], out[:, w - t :], TN
                    )

        return carry

    lax.fori_loop(0, steps, step, 0)


def factor(g, coupling):
    order = coupling.shape[0]
    return pl.pallas_call(
        factor_kernel,
        out_shape=jax.ShapeDtypeStruct((order, order), F32),
        in_specs=[VMEM] * 2,
        out_specs=VMEM,
        scratch_shapes=[
            pltpu.VMEM((order, 2 * order), F32),
            pltpu.VMEM((NB, NB), F32),
            pltpu.VMEM((W * W, NB), F32),
            pltpu.VMEM((W, NB), F32),
            pltpu.VMEM((W, NB), F32),
        ],
        name="factor",
        cost_estimate=pl.CostEstimate(flops=2_000_000_000, bytes_accessed=3 << 20, transcendentals=0),
    )(g, coupling)


def level_kernel(levels, m, q, sums, half, v, h):
    r = m.shape[0] // 2
    ms = split2(m[...])
    ps = split2(dot3(ms, split2(q[...]), NN))
    own = split2(m[:, pl.ds(pl.multiple_of(half[0] * r, r), r)])
    v[...] = dot3(own, ps, TN)
    at = 0
    for i in range(levels):
        left = tuple(x[:, i * r : (i + 1) * r] for x in ps)
        for j in range(i, levels + 1):
            right = tuple(x[:, j * r : (j + 1) * r] for x in ps)
            h[:, at : at + r] = sums[:, at : at + r] - dot3(left, right, TN)
            at += r


def level_update(levels, m, q, sums, half):
    r = m.shape[0] // 2
    wide = (levels + 1) * r
    return pl.pallas_call(
        lambda *refs: level_kernel(levels, *refs),
        out_shape=[jax.ShapeDtypeStruct((r, wide), F32), jax.ShapeDtypeStruct(sums.shape, F32)],
        in_specs=[VMEM] * 3 + [pl.BlockSpec(memory_space=pltpu.SMEM)],
        out_specs=[VMEM, VMEM],
        name="level_update",
    )(m, q, sums, half)


def back_kernel(m, q, half, v3, v2, x):
    r = m.shape[0] // 2
    ps = dot3(split2(m[...]), split2(q[...]), NN)
    x1 = dot3(split2(m[:, pl.ds(pl.multiple_of(half[0] * r, r), r)]), split2(ps), TN)
    s1 = split2(x1)
    x2 = v2[:, r:] - dot3(split2(v2[:, :r]), s1, NN)
    s2 = split2(x2)
    x3 = v3[:, 2 * r :] - dot3(split2(v3[:, :r]), s2, NN) - dot3(split2(v3[:, r : 2 * r]), s1, NN)
    x[:r, :] = x3
    x[r : 2 * r, :] = x2
    x[2 * r :, :] = x1


def back(m, q, half, v3, v2):
    r = m.shape[0] // 2
    return pl.pallas_call(
        back_kernel,
        out_shape=jax.ShapeDtypeStruct((3 * r, r), F32),
        in_specs=[VMEM] * 2 + [pl.BlockSpec(memory_space=pltpu.SMEM)] + [VMEM] * 2,
        out_specs=VMEM,
        name="back",
    )(m, q, half, v3, v2)


def apply_kernel(b3, b2, b1, rhs, leaf, x, out):
    r = b3.shape[1]
    xs = split2(x[...])
    total = rhs[...]
    for i, b in enumerate((b3, b2, b1)):
        total = total - dot3(split2(b[...]), tuple(y[i * r : (i + 1) * r] for y in xs), NN)
    out[...] = total * leaf[...]


def apply_update(b3, b2, b1, rhs, leaf, x):
    rows, r = b3.shape
    tile = 512
    block = pl.BlockSpec((tile, r), lambda i: (i, 0))
    return pl.pallas_call(
        apply_kernel,
        grid=(rows // tile,),
        in_specs=[block] * 4
        + [pl.BlockSpec((tile, 1), lambda i: (i, 0)), pl.BlockSpec(x.shape, lambda i: (0, 0))],
        out_specs=block,
        out_shape=jax.ShapeDtypeStruct(rhs.shape, F32),
        name="apply_update",
    )(b3, b2, b1, rhs, leaf[:, None], x)


def core_rows(m, offset, count):
    own = lax.dynamic_slice_in_dim(m, offset, count, 1)
    return lax.dot_general(
        own, m, (TN, ((), ())), precision=lax.Precision.HIGHEST, preferred_element_type=F32
    )


def per_device(basis3, basis2, basis1, leaf_inverse, rhs, coupling3, coupling2, coupling1):
    r = basis3.shape[1]
    nx = lax.axis_size("gx")
    ny = lax.axis_size("gy")
    devices = nx * ny
    gx = lax.axis_index("gx")
    place = gx * ny + lax.axis_index("gy")

    def sibling(value, bit):
        return lax.ppermute(value, "gx", [(s, s ^ (1 << bit)) for s in range(nx)])

    def ordered(value, other, bit):
        low = (gx >> bit) & 1 == 0
        return jnp.concatenate(
            [jnp.where(low, value, other), jnp.where(low, other, value)], axis=0
        )

    first, rest = grams(basis3, basis2, basis1, rhs, leaf_inverse)
    first = lax.psum(first, "gy")
    g3 = ordered(first, sibling(first, 0), 0)
    rest = lax.psum(rest, "gy")
    rest_other = sibling(rest, 0)
    q3 = ordered(rest[:, : 3 * r], rest_other[:, : 3 * r], 0)
    sums = rest[:, 3 * r :] + rest_other[:, 3 * r :]

    pair3 = lax.dynamic_index_in_dim(coupling3, gx >> 1, 0, keepdims=False)
    m3 = factor(g3, pair3)
    v3, h2 = level_update(2, m3, q3, sums, (gx & 1).reshape(1))
    h2_other = sibling(h2[:, : 3 * r], 1)
    g2 = ordered(h2[:, :r], h2_other[:, :r], 1)
    q2 = ordered(h2[:, r : 3 * r], h2_other[:, r : 3 * r], 1)
    tail = h2[:, 3 * r :]
    sums1 = tail + sibling(tail, 1)

    pair2 = lax.dynamic_index_in_dim(coupling2, gx >> 2, 0, keepdims=False)
    m2 = factor(g2, pair2)
    v2, h1 = level_update(1, m2, q2, sums1, ((gx >> 1) & 1).reshape(1))
    h1_other = sibling(h1, 2)
    g1 = ordered(h1[:, :r], h1_other[:, :r], 2)
    q1 = ordered(h1[:, r:], h1_other[:, r:], 2)
    m1 = factor(g1, coupling1[0])
    x = back(m1, q1, (gx >> 2).reshape(1), v3, v2)
    solved = apply_update(basis3, basis2, basis1, rhs, leaf_inverse, x)
    cores = []
    for level, m in ((3, m3), (2, m2), (1, m1)):
        count = 2**level * r // devices
        group = devices >> (level - 1)
        cores.append(core_rows(m, (place % group) * count, count))
    return (solved, *cores)


def solution(mesh):
    rows = P(("gx", "gy"), None)
    return jax.shard_map(
        per_device,
        mesh=mesh,
        in_specs=(rows, rows, rows, P(("gx", "gy")), rows, P(), P(), P()),
        out_specs=(rows, rows, rows, rows),
        check_vma=False,
    )
```

```python
import jax
import jax.numpy as jnp
from jax import lax
from jax.experimental import pallas as pl
from jax.experimental.pallas import tpu as pltpu
from jax.sharding import PartitionSpec as P

F32 = jnp.float32
BF16 = jnp.bfloat16
NN = ((1,), (0,))
TN = ((0,), (0,))
W = 32
NB = 128
VMEM = pl.BlockSpec(memory_space=pltpu.VMEM)


def dot6(a, b, dims):
    return lax.dot_general(
        a, b, (dims, ((), ())), precision=lax.Precision.HIGHEST, preferred_element_type=F32
    )


def dot1(a, b, dims):
    return lax.dot_general(a, b, (dims, ((), ())), preferred_element_type=F32)


def split2(x):
    hi = x.astype(BF16)
    return hi, (x - hi.astype(F32)).astype(BF16)


def split3(x):
    hi = x.astype(BF16)
    rest = x - hi.astype(F32)
    mid = rest.astype(BF16)
    return hi, mid, (rest - mid.astype(F32)).astype(BF16)


def dot3(a, b, dims):
    (i,), (j,) = dims
    left = jnp.concatenate([a[0], a[0], a[1]], i)
    right = jnp.concatenate([b[0], b[1], b[0]], j)
    return dot1(left, right, dims)


MESH = pl.DeviceIdType.MESH


def where_am_i():
    gx = lax.axis_index("gx")
    gy = lax.axis_index("gy")
    core = gy % 2
    return gx, gy, core, gy // 2, gy + 1 - 2 * core, gx + 1 - 2 * (gx % 2)


def enter(peers):
    barrier = pltpu.get_barrier_semaphore()
    for peer in peers:
        pl.semaphore_signal(barrier, inc=1, device_id=peer, device_id_type=MESH)
    pl.semaphore_wait(barrier, len(peers))


def group_peers(chips):
    gx, gy, core, chip, other, sib = where_am_i()
    own = [(gx, 2 * ((chip + d) % chips) + core) for d in range(1, chips)]
    far = [(sib, 2 * ((chip + d) % chips) + core) for d in range(chips)]
    return [(gx, other)] + own + far


def remote(src, dst, send, recv, peer):
    return pltpu.make_async_remote_copy(
        src_ref=src, dst_ref=dst, send_sem=send, recv_sem=recv, device_id=peer, device_id_type=MESH
    )


GROUPS = (((0, 0),), ((0, 1), (1, 1)), ((0, 2), (1, 2), (2, 2)), ((0, 3), (1, 3), (2, 3)))
TILE = 256


def gram_reduce_kernel(
    chips, b3, b2, b1, rhs, leaf, g, qp, sp, raw, hi, lo, part, near, half, arrived, piece, far,
    load_sem, near_sem, rs_sem, ag_sem, share_sem, far_sem,
):
    gx, gy, core, chip, other, sib = where_am_i()
    side = gx % 2
    rows, r = b3.shape
    tiles = rows // TILE
    lanes = leaf.shape[1]
    per = TILE // lanes
    hr = r // 2
    pr = hr // chips
    loads = [
        pltpu.make_async_copy(b, raw.at[i], load_sem.at[i]) for i, b in enumerate((b3, b2, b1, rhs))
    ]
    for copy in loads:
        copy.start()
    peers = group_peers(chips)
    enter(peers)
    own_peers = peers[1:chips]
    far_peers = peers[chips:]
    root = jnp.sqrt(leaf[...]).T
    partner = (gx, other)

    def local(i):
        loads[i].wait()
        for t in range(tiles):
            scale = jnp.concatenate([root[:, t * per + u : t * per + u + 1] for u in range(per)], 0)
            h, l = split2(raw[i, t * TILE : (t + 1) * TILE, :] * scale)
            hi[i, t * TILE : (t + 1) * TILE, :] = h
            lo[i, t * TILE : (t + 1) * TILE, :] = l
        for n, (p, q) in enumerate(GROUPS[i]):
            part[i, n] = jnp.zeros((r, r), F32)

        def tile(t, carry):
            at = pl.ds(pl.multiple_of(t * TILE, TILE), TILE)
            for n, (p, q) in enumerate(GROUPS[i]):
                part[i, n] += dot3((hi[p, at, :], lo[p, at, :]), (hi[q, at, :], lo[q, at, :]), TN)
            return carry

        lax.fori_loop(0, tiles, tile, 0)
        n = len(GROUPS[i])
        copy = remote(
            part.at[i, pl.ds(0, n), pl.ds((1 - core) * hr, hr), :],
            near.at[i, pl.ds(0, n)],
            near_sem.at[0, i], near_sem.at[1, i], partner,
        )
        copy.start()
        return copy

    def scatter(i, copy):
        n = len(GROUPS[i])
        copy.wait_recv()
        mine = pl.ds(pl.multiple_of(core * hr, hr), hr)
        half[i, 0:n] = part[i, 0:n, mine, :] + near[i, 0:n]
        out = []
        for d in range(1, chips):
            to = pl.ds(pl.multiple_of(((chip + d) % chips) * pr, pr), pr)
            out.append(
                remote(
                    half.at[i, pl.ds(0, n), to, :],
                    arrived.at[i, d - 1, pl.ds(0, n)],
                    rs_sem.at[0, i, d - 1], rs_sem.at[1, i, d - 1], own_peers[d - 1],
                )
            )
            out[-1].start()
        return out

    def collect(i, copies):
        n = len(GROUPS[i])
        total = half[i, 0:n, pl.ds(pl.multiple_of(chip * pr, pr), pr), :]
        for d, copy in enumerate(copies):
            copy.wait_recv()
            total = total + arrived[i, d, 0:n]
        piece[i, 0:n] = total

    near0 = local(0)
    near1 = local(1)
    rs0 = scatter(0, near0)
    near2 = local(2)
    collect(0, rs0)
    row = pl.multiple_of(side * r + core * hr + chip * pr, pr)
    g[pl.ds(row, pr), :] = piece[0, 0]
    ag = []
    for d, peer in enumerate(own_peers + far_peers):
        ag.append(
            remote(piece.at[0, 0], g.at[pl.ds(row, pr), :], ag_sem.at[0, d], ag_sem.at[1, d], peer)
        )
        ag[-1].start()
    rs1 = scatter(1, near1)
    near3 = local(3)
    rs2 = scatter(2, near2)
    for copy in ag:
        copy.wait_recv()
    shares = []
    for s in range(2):
        at = pl.ds(pl.multiple_of(s * r + core * hr, hr), hr)
        shares.append(remote(g.at[at, :], g.at[at, :], share_sem.at[0, s], share_sem.at[1, s], partner))
        shares[-1].start()
    rs3 = scatter(3, near3)
    across = []
    for i, copies in ((1, rs1), (2, rs2), (3, rs3)):
        collect(i, copies)
        n = len(GROUPS[i]) - 1
        across.append(
            remote(
                piece.at[i, pl.ds(1, n)], far.at[i, pl.ds(0, n)],
                far_sem.at[0, i], far_sem.at[1, i], (sib, gy),
            )
        )
        across[-1].start()
        qp[:, (i - 1) * r : i * r] = piece[i, 0]
    keep = pl.ds(pl.multiple_of(side * (pr // 2), pr // 2), pr // 2)
    order = {(1, 0): 0, (2, 0): 1, (3, 0): 2, (2, 1): 3, (3, 1): 4}
    for i, copy in zip((1, 2, 3), across):
        copy.wait_recv()
        for n in range(len(GROUPS[i]) - 1):
            at = order[i, n] * r
            sp[:, at : at + r] = piece[i, n + 1, keep, :] + far[i, n, keep, :]
    for copy in shares:
        copy.wait_recv()
    for copy in [near0, near1, near2, near3, *rs0, *rs1, *rs2, *rs3, *ag, *shares, *across]:
        copy.wait_send()


def gram_reduce(b3, b2, b1, rhs, leaf):
    rows, r = b3.shape
    chips = lax.axis_size("gy") // 2
    hr = r // 2
    pr = hr // chips
    most = max(len(x) for x in GROUPS)
    count = len(GROUPS)
    hbm = pl.BlockSpec(memory_space=pl.ANY)
    dma = pltpu.SemaphoreType.DMA
    return pl.pallas_call(
        lambda *refs: gram_reduce_kernel(chips, *refs),
        in_specs=[hbm] * 4 + [VMEM],
        out_specs=[VMEM] * 3,
        out_shape=[
            jax.ShapeDtypeStruct((2 * r, r), F32),
            jax.ShapeDtypeStruct((pr, 3 * r), F32),
            jax.ShapeDtypeStruct((pr // 2, 5 * r), F32),
        ],
        scratch_shapes=[
            pltpu.VMEM((4, rows, r), F32),
            pltpu.VMEM((4, rows, r), BF16),
            pltpu.VMEM((4, rows, r), BF16),
            pltpu.VMEM((count, most, r, r), F32),
            pltpu.VMEM((count, most, hr, r), F32),
            pltpu.VMEM((count, most, hr, r), F32),
            pltpu.VMEM((count, chips - 1, most, pr, r), F32),
            pltpu.VMEM((count, most, pr, r), F32),
            pltpu.VMEM((count, most - 1, pr, r), F32),
            dma((4,)),
            dma((2, count)),
            dma((2, count, chips - 1)),
            dma((2, 2 * chips - 1)),
            dma((2, 2)),
            dma((2, count)),
        ],
        compiler_params=pltpu.CompilerParams(
            collective_id=0, has_side_effects=True, vmem_limit_bytes=48 << 20
        ),
        name="gram_reduce",
    )(b3, b2, b1, rhs, leaf.reshape(rows // 128, 128))


def invert_factor(work):
    n = work.shape[0]
    lane = lax.broadcasted_iota(jnp.int32, (W, n), 1)
    sub = lax.broadcasted_iota(jnp.int32, (W, n), 0)
    for s in range(n // W):
        o = s * W
        block = work[o : o + W, :]
        cols = [
            jnp.stack(
                [
                    jnp.broadcast_to(block[8 * h :, o + k : o + k + 1], (W - 8 * h, n))
                    for k in range(8 * h, 8 * h + 8)
                ],
                0,
            )
            for h in range(W // 8)
        ]
        x = jnp.where((lane >= o) & (lane < o + W), jnp.where(lane - o == sub, 1.0, 0.0), block)
        for k in range(W):
            first = k // 8
            low = sub[8 * first :]
            column = cols[first][k % 8]
            d = column[k % 8 : k % 8 + 1]
            m = jnp.where(low > k, column * (1.0 / d), 0.0)
            for h in range(first, W // 8):
                from_h = 8 * (h - first)
                cols[h] = cols[h] - m[from_h:][None] * column[from_h : from_h + 8][:, None, :]
            tail = x[8 * first :]
            tail = tail - m * x[k : k + 1]
            tail = jnp.where(low == k, tail * lax.rsqrt(d), tail)
            x = tail if first == 0 else jnp.concatenate([x[: 8 * first], tail], 0)
        work[o : o + W, :] = jnp.where(lane < o + W, x, 0.0)
        t = o + W
        if t < n:
            v1, v2, v3 = split3(x)
            left = jnp.concatenate([v1, v1, v2, v1, v3, v2], 0)
            right = jnp.concatenate([v1, v2, v1, v3, v1, v2], 0)
            update = dot1(left, right, TN)
            below = lax.broadcasted_iota(jnp.int32, (n - t, n), 1)
            kept = jnp.where((below >= o) & (below < t), 0.0, work[t:, :])
            work[t:, :] = kept - update[t:, :]


def factor_kernel(g, coupling, m, c, work, between=None):
    r = g.shape[1]
    order = 2 * r
    steps = order // NB
    gl = jnp.concatenate(
        [dot6(g[:r, :], coupling[:r, :], NN), dot6(g[r:, :], coupling[r:, :], NN)], 0
    )
    eye = jnp.where(
        lax.broadcasted_iota(jnp.int32, (NB, NB), 0) == lax.broadcasted_iota(jnp.int32, (NB, NB), 1),
        1.0,
        0.0,
    )
    full = coupling[...]
    for j in range(steps):
        o = j * NB
        c[o : o + NB, o:order] = dot6(full[:, o : o + NB], gl[:, o:], TN)
        c[o : o + NB, order:] = full[:, o : o + NB].T

    def step(j, carry):
        for jj in range(steps):

            @pl.when(j == jj)
            def _(o=jj * NB):
                work[...] = c[o : o + NB, o : o + NB] + eye

        invert_factor(work)
        for jj in range(steps):

            @pl.when(j == jj)
            def _(jj=jj, o=jj * NB, t=jj * NB + NB):
                out = dot6(work[...], c[o : o + NB, t:], NN)
                m[o : o + NB, :] = out[:, order - t :]
                for q in range(jj + 1, steps):
                    w = q * NB
                    c[w : w + NB, w:] = c[w : w + NB, w:] - dot6(
                        out[:, w - t : w - t + NB], out[:, w - t :], TN
                    )
                if between is not None:
                    between(jj)

        return carry

    lax.fori_loop(0, steps, step, 0)


def factor(g, coupling):
    order = coupling.shape[0]
    return pl.pallas_call(
        factor_kernel,
        out_shape=jax.ShapeDtypeStruct((order, order), F32),
        in_specs=[VMEM] * 2,
        out_specs=VMEM,
        scratch_shapes=[
            pltpu.VMEM((order, 2 * order), F32),
            pltpu.VMEM((NB, NB), F32),
        ],
        name="factor",
        cost_estimate=pl.CostEstimate(flops=2_000_000_000, bytes_accessed=3 << 20, transcendentals=0),
    )(g, coupling)


def factor_gather_kernel(
    chips, g, coupling, qp, sp, m, q, s, c, work, q_sem, s_sem, share_sem
):
    gx, gy, core, chip, other, sib = where_am_i()
    side = gx % 2
    pr = qp.shape[0]
    hr = pr * chips
    peers = group_peers(chips)
    enter(peers)
    q_row = pl.multiple_of(side * 2 * hr + core * hr + chip * pr, pr)
    s_row = pl.multiple_of(core * hr + chip * pr + side * (pr // 2), pr // 2)
    q_at = q.at[pl.ds(q_row, pr), :]
    s_at = s.at[pl.ds(s_row, pr // 2), :]
    gathers = []
    for d, peer in enumerate(peers[1:]):
        gathers.append(remote(qp, q_at, q_sem.at[0, d], q_sem.at[1, d], peer))
        gathers.append(remote(sp, s_at, s_sem.at[0, d], s_sem.at[1, d], peer))
    for copy in gathers:
        copy.start()
    q[pl.ds(q_row, pr), :] = qp[...]
    s[pl.ds(s_row, pr // 2), :] = sp[...]
    shares = []
    for n, (ref, at) in enumerate(((q, core * hr), (q, 2 * hr + core * hr), (s, core * hr))):
        at = ref.at[pl.ds(pl.multiple_of(at, hr), hr), :]
        shares.append(remote(at, at, share_sem.at[0, n], share_sem.at[1, n], (gx, other)))

    def between(jj):
        if jj == 2:
            for copy in gathers:
                copy.wait_recv()
            for copy in shares:
                copy.start()

    factor_kernel(g, coupling, m, c, work, between)
    for copy in shares:
        copy.wait()
    for copy in gathers:
        copy.wait_send()


def factor_gather(g, coupling, qp, sp):
    order = coupling.shape[0]
    chips = lax.axis_size("gy") // 2
    dma = pltpu.SemaphoreType.DMA
    return pl.pallas_call(
        lambda *refs: factor_gather_kernel(chips, *refs),
        out_shape=[
            jax.ShapeDtypeStruct((order, order), F32),
            jax.ShapeDtypeStruct((order, qp.shape[1]), F32),
            jax.ShapeDtypeStruct((order // 2, sp.shape[1]), F32),
        ],
        in_specs=[VMEM] * 4,
        out_specs=[VMEM] * 3,
        scratch_shapes=[
            pltpu.VMEM((order, 2 * order), F32),
            pltpu.VMEM((NB, NB), F32),
            dma((2, 2 * chips - 1)),
            dma((2, 2 * chips - 1)),
            dma((2, 3)),
        ],
        compiler_params=pltpu.CompilerParams(
            collective_id=1, has_side_effects=True, vmem_limit_bytes=48 << 20
        ),
        name="factor_gather",
    )(g, coupling, qp, sp)


def level_kernel(levels, m, q, sums, half, v, h):
    r = m.shape[0] // 2
    ms = split2(m[...])
    ps = split2(dot3(ms, split2(q[...]), NN))
    own = split2(m[:, pl.ds(pl.multiple_of(half[0] * r, r), r)])
    v[...] = dot3(own, ps, TN)
    at = 0
    for i in range(levels):
        left = tuple(x[:, i * r : (i + 1) * r] for x in ps)
        for j in range(i, levels + 1):
            right = tuple(x[:, j * r : (j + 1) * r] for x in ps)
            h[:, at : at + r] = sums[:, at : at + r] - dot3(left, right, TN)
            at += r


def level_update(levels, m, q, sums, half):
    r = m.shape[0] // 2
    wide = (levels + 1) * r
    return pl.pallas_call(
        lambda *refs: level_kernel(levels, *refs),
        out_shape=[jax.ShapeDtypeStruct((r, wide), F32), jax.ShapeDtypeStruct(sums.shape, F32)],
        in_specs=[VMEM] * 3 + [pl.BlockSpec(memory_space=pltpu.SMEM)],
        out_specs=[VMEM, VMEM],
        name="level_update",
    )(m, q, sums, half)


def back_kernel(m, q, half, v3, v2, x):
    r = m.shape[0] // 2
    ps = dot3(split2(m[...]), split2(q[...]), NN)
    x1 = dot3(split2(m[:, pl.ds(pl.multiple_of(half[0] * r, r), r)]), split2(ps), TN)
    s1 = split2(x1)
    x2 = v2[:, r:] - dot3(split2(v2[:, :r]), s1, NN)
    s2 = split2(x2)
    x3 = v3[:, 2 * r :] - dot3(split2(v3[:, :r]), s2, NN) - dot3(split2(v3[:, r : 2 * r]), s1, NN)
    x[:r, :] = x3
    x[r : 2 * r, :] = x2
    x[2 * r :, :] = x1


def back(m, q, half, v3, v2):
    r = m.shape[0] // 2
    return pl.pallas_call(
        back_kernel,
        out_shape=jax.ShapeDtypeStruct((3 * r, r), F32),
        in_specs=[VMEM] * 2 + [pl.BlockSpec(memory_space=pltpu.SMEM)] + [VMEM] * 2,
        out_specs=VMEM,
        name="back",
    )(m, q, half, v3, v2)


def apply_kernel(b3, b2, b1, rhs, leaf, x, out):
    r = b3.shape[1]
    xs = split2(x[...])
    total = rhs[...]
    for i, b in enumerate((b3, b2, b1)):
        total = total - dot3(split2(b[...]), tuple(y[i * r : (i + 1) * r] for y in xs), NN)
    out[...] = total * leaf[...]


def apply_update(b3, b2, b1, rhs, leaf, x):
    rows, r = b3.shape
    tile = 512
    block = pl.BlockSpec((tile, r), lambda i: (i, 0))
    return pl.pallas_call(
        apply_kernel,
        grid=(rows // tile,),
        in_specs=[block] * 4
        + [pl.BlockSpec((tile, 1), lambda i: (i, 0)), pl.BlockSpec(x.shape, lambda i: (0, 0))],
        out_specs=block,
        out_shape=jax.ShapeDtypeStruct(rhs.shape, F32),
        name="apply_update",
    )(b3, b2, b1, rhs, leaf[:, None], x)


def core_rows(m, offset, count):
    own = lax.dynamic_slice_in_dim(m, offset, count, 1)
    return lax.dot_general(
        own, m, (TN, ((), ())), precision=lax.Precision.HIGHEST, preferred_element_type=F32
    )


def per_device(basis3, basis2, basis1, leaf_inverse, rhs, coupling3, coupling2, coupling1):
    r = basis3.shape[1]
    nx = lax.axis_size("gx")
    ny = lax.axis_size("gy")
    devices = nx * ny
    gx = lax.axis_index("gx")
    place = gx * ny + lax.axis_index("gy")

    def sibling(value, bit):
        return lax.ppermute(value, "gx", [(s, s ^ (1 << bit)) for s in range(nx)])

    def ordered(value, other, bit):
        low = (gx >> bit) & 1 == 0
        return jnp.concatenate(
            [jnp.where(low, value, other), jnp.where(low, other, value)], axis=0
        )

    pair3 = lax.dynamic_index_in_dim(coupling3, gx >> 1, 0, keepdims=False)
    g3, q_piece, s_piece = gram_reduce(basis3, basis2, basis1, rhs, leaf_inverse)
    m3, q3, sums = factor_gather(g3, pair3, q_piece, s_piece)
    v3, h2 = level_update(2, m3, q3, sums, (gx & 1).reshape(1))
    g2 = ordered(h2[:, :r], sibling(h2[:, :r], 1), 1)
    q2 = ordered(h2[:, r : 3 * r], sibling(h2[:, r : 3 * r], 1), 1)
    tail = h2[:, 3 * r :]
    sums1 = tail + sibling(tail, 1)

    pair2 = lax.dynamic_index_in_dim(coupling2, gx >> 2, 0, keepdims=False)
    m2 = factor(g2, pair2)
    v2, h1 = level_update(1, m2, q2, sums1, ((gx >> 1) & 1).reshape(1))
    h1_other = sibling(h1, 2)
    g1 = ordered(h1[:, :r], h1_other[:, :r], 2)
    q1 = ordered(h1[:, r:], h1_other[:, r:], 2)
    m1 = factor(g1, coupling1[0])
    x = back(m1, q1, (gx >> 2).reshape(1), v3, v2)
    solved = apply_update(basis3, basis2, basis1, rhs, leaf_inverse, x)
    cores = []
    for level, m in ((3, m3), (2, m2), (1, m1)):
        count = 2**level * r // devices
        group = devices >> (level - 1)
        cores.append(core_rows(m, (place % group) * count, count))
    return (solved, *cores)


def solution(mesh):
    rows = P(("gx", "gy"), None)
    return jax.shard_map(
        per_device,
        mesh=mesh,
        in_specs=(rows, rows, rows, P(("gx", "gy")), rows, P(), P(), P()),
        out_specs=(rows, rows, rows, rows),
        check_vma=False,
    )
```

```python
import jax
import jax.numpy as jnp
from jax import lax
from jax.experimental import pallas as pl
from jax.experimental.pallas import tpu as pltpu
from jax.sharding import PartitionSpec as P

F32 = jnp.float32
BF16 = jnp.bfloat16
NN = ((1,), (0,))
TN = ((0,), (0,))
W = 32
NB = 128
VMEM = pl.BlockSpec(memory_space=pltpu.VMEM)


def dot6(a, b, dims):
    return lax.dot_general(
        a, b, (dims, ((), ())), precision=lax.Precision.HIGHEST, preferred_element_type=F32
    )


def dot1(a, b, dims):
    return lax.dot_general(a, b, (dims, ((), ())), preferred_element_type=F32)


def split2(x):
    hi = x.astype(BF16)
    return hi, (x - hi.astype(F32)).astype(BF16)


def split3(x):
    hi = x.astype(BF16)
    rest = x - hi.astype(F32)
    mid = rest.astype(BF16)
    return hi, mid, (rest - mid.astype(F32)).astype(BF16)


def dot3(a, b, dims):
    (i,), (j,) = dims
    left = jnp.concatenate([a[0], a[0], a[1]], i)
    right = jnp.concatenate([b[0], b[1], b[0]], j)
    return dot1(left, right, dims)


MESH = pl.DeviceIdType.MESH


def where_am_i():
    gx = lax.axis_index("gx")
    gy = lax.axis_index("gy")
    core = gy % 2
    return gx, gy, core, gy // 2, gy + 1 - 2 * core, gx + 1 - 2 * (gx % 2)


def enter(peers):
    barrier = pltpu.get_barrier_semaphore()
    for peer in peers:
        pl.semaphore_signal(barrier, inc=1, device_id=peer, device_id_type=MESH)
    pl.semaphore_wait(barrier, len(peers))


def group_peers(chips):
    gx, gy, core, chip, other, sib = where_am_i()
    own = [(gx, 2 * ((chip + d) % chips) + core) for d in range(1, chips)]
    far = [(sib, 2 * ((chip + d) % chips) + core) for d in range(chips)]
    return [(gx, other)] + own + far


def remote(src, dst, send, recv, peer):
    return pltpu.make_async_remote_copy(
        src_ref=src, dst_ref=dst, send_sem=send, recv_sem=recv, device_id=peer, device_id_type=MESH
    )


def invert_factor(work):
    n = work.shape[0]
    lane = lax.broadcasted_iota(jnp.int32, (W, n), 1)
    sub = lax.broadcasted_iota(jnp.int32, (W, n), 0)
    for s in range(n // W):
        o = s * W
        block = work[o : o + W, :]
        cols = [
            jnp.stack(
                [
                    jnp.broadcast_to(block[8 * h :, o + k : o + k + 1], (W - 8 * h, n))
                    for k in range(8 * h, 8 * h + 8)
                ],
                0,
            )
            for h in range(W // 8)
        ]
        x = jnp.where((lane >= o) & (lane < o + W), jnp.where(lane - o == sub, 1.0, 0.0), block)
        for k in range(W):
            first = k // 8
            low = sub[8 * first :]
            column = cols[first][k % 8]
            d = column[k % 8 : k % 8 + 1]
            m = jnp.where(low > k, column * (1.0 / d), 0.0)
            for h in range(first, W // 8):
                from_h = 8 * (h - first)
                cols[h] = cols[h] - m[from_h:][None] * column[from_h : from_h + 8][:, None, :]
            tail = x[8 * first :]
            tail = tail - m * x[k : k + 1]
            tail = jnp.where(low == k, tail * lax.rsqrt(d), tail)
            x = tail if first == 0 else jnp.concatenate([x[: 8 * first], tail], 0)
        work[o : o + W, :] = jnp.where(lane < o + W, x, 0.0)
        t = o + W
        if t < n:
            v1, v2, v3 = split3(x)
            left = jnp.concatenate([v1, v1, v2, v1, v3, v2], 0)
            right = jnp.concatenate([v1, v2, v1, v3, v1, v2], 0)
            update = dot1(left, right, TN)
            below = lax.broadcasted_iota(jnp.int32, (n - t, n), 1)
            kept = jnp.where((below >= o) & (below < t), 0.0, work[t:, :])
            work[t:, :] = kept - update[t:, :]


GROUPS = (((0, 0),), ((0, 1), (1, 1)), ((0, 2), (1, 2), (2, 2)), ((0, 3), (1, 3), (2, 3)))
ORDER = {(1, 0): 0, (2, 0): 1, (2, 1): 3, (3, 0): 2, (3, 1): 4}
TILE = 256


def mega_kernel(
    chips, b3, b2, b1, rhs, leaf, cpl3, cpl2, cpl1, x, core3, core2, core1,
    raw, hi, lo, part, near, half, arrived, piece, far, pay, bag, g, q, s, h, q1, s1, tail, q2,
    coupling, c, work, m, p, v3, v2, krows,
    load_sem, near_sem, rs_sem, ag_sem, share_sem, far_sem, bag_sem, bshare_sem, ex_sem, exs_sem,
):
    gx, gy, core, chip, other, sib = where_am_i()
    rows, r = b3.shape
    order = 2 * r
    tiles = rows // TILE
    per = TILE // leaf.shape[1]
    hr = r // 2
    pr = hr // chips
    sides = (gx % 2, (gx // 2) % 2, (gx // 4) % 2)
    far_gx = (sib, gx + 2 - 4 * sides[1], gx + 4 - 8 * sides[2])
    side = sides[0]
    partner = (gx, other)

    loads = [
        pltpu.make_async_copy(b, raw.at[i], load_sem.at[i]) for i, b in enumerate((b3, b2, b1, rhs))
    ]
    loads += [
        pltpu.make_async_copy(src.at[at], coupling.at[i], load_sem.at[4 + i])
        for i, (src, at) in enumerate(((cpl3, gx // 2), (cpl2, gx // 4), (cpl1, 0)))
    ]
    for copy in loads:
        copy.start()
    peers = group_peers(chips)
    enter(peers + [(far_gx[1], gy), (far_gx[2], gy)])
    root = jnp.sqrt(leaf[...]).T

    nears = [
        remote(
            part.at[i, pl.ds(0, len(GROUPS[i])), pl.ds(pl.multiple_of((1 - core) * hr, hr), hr), :],
            near.at[i, pl.ds(0, len(GROUPS[i]))],
            near_sem.at[0, i], near_sem.at[1, i], partner,
        )
        for i in range(4)
    ]
    scatters = [
        [
            remote(
                half.at[
                    i, pl.ds(0, len(GROUPS[i])),
                    pl.ds(pl.multiple_of(((chip + d) % chips) * pr, pr), pr), :,
                ],
                arrived.at[i, d - 1, pl.ds(0, len(GROUPS[i]))],
                rs_sem.at[0, i, d - 1], rs_sem.at[1, i, d - 1], peers[d],
            )
            for d in range(1, chips)
        ]
        for i in range(4)
    ]
    row = pl.multiple_of(side * r + core * hr + chip * pr, pr)
    g_gather = [
        remote(
            piece.at[0, 0], g.at[0, pl.ds(row, pr), :], ag_sem.at[0, d], ag_sem.at[1, d], peer
        )
        for d, peer in enumerate(peers[1:])
    ]
    g_shares = []
    for t in range(2):
        at = g.at[0, pl.ds(pl.multiple_of(t * r + core * hr, hr), hr), :]
        g_shares.append(remote(at, at, share_sem.at[0, t], share_sem.at[1, t], partner))
    across = [
        remote(
            piece.at[i, pl.ds(1, len(GROUPS[i]) - 1)], far.at[i, pl.ds(0, len(GROUPS[i]) - 1)],
            far_sem.at[0, i], far_sem.at[1, i], (sib, gy),
        )
        for i in range(1, 4)
    ]
    bag_rows = [pr + (pr // 2) * (len(GROUPS[i]) - 1) for i in range(1, 4)]
    gathers = [
        [
            remote(
                pay.at[i, pl.ds(0, n), :], bag.at[i, side, core, chip, pl.ds(0, n), :],
                bag_sem.at[0, i, d], bag_sem.at[1, i, d], peer,
            )
            for d, peer in enumerate(peers[1:])
        ]
        for i, n in enumerate(bag_rows)
    ]
    bag_shares = [
        [
            remote(
                bag.at[i, t, core, :, pl.ds(0, n), :], bag.at[i, t, core, :, pl.ds(0, n), :],
                bshare_sem.at[0, i, t], bshare_sem.at[1, i, t], partner,
            )
            for t in range(2)
        ]
        for i, n in enumerate(bag_rows)
    ]

    def local(i):
        loads[i].wait()
        for t in range(tiles):
            scale = jnp.concatenate([root[:, t * per + u : t * per + u + 1] for u in range(per)], 0)
            upper, lower = split2(raw[i, t * TILE : (t + 1) * TILE, :] * scale)
            hi[i, t * TILE : (t + 1) * TILE, :] = upper
            lo[i, t * TILE : (t + 1) * TILE, :] = lower
        for n in range(len(GROUPS[i])):
            part[i, n] = jnp.zeros((r, r), F32)

        def tile(t, carry):
            at = pl.ds(pl.multiple_of(t * TILE, TILE), TILE)
            for n, (a, b) in enumerate(GROUPS[i]):
                part[i, n] += dot3((hi[a, at, :], lo[a, at, :]), (hi[b, at, :], lo[b, at, :]), TN)
            return carry

        lax.fori_loop(0, tiles, tile, 0)
        nears[i].start()

    def scatter(i):
        n = len(GROUPS[i])
        nears[i].wait_recv()
        half[i, 0:n] = part[i, 0:n, pl.ds(pl.multiple_of(core * hr, hr), hr), :] + near[i, 0:n]
        for copy in scatters[i]:
            copy.start()

    def collect(i):
        n = len(GROUPS[i])
        total = half[i, 0:n, pl.ds(pl.multiple_of(chip * pr, pr), pr), :]
        for d, copy in enumerate(scatters[i]):
            copy.wait_recv()
            total = total + arrived[i, d, 0:n]
        piece[i, 0:n] = total
        if i > 0:
            across[i - 1].start()

    def gather(i):
        across[i - 1].wait_recv()
        pay[i - 1, 0:pr, :] = piece[i, 0]
        keep = pl.ds(pl.multiple_of(side * (pr // 2), pr // 2), pr // 2)
        for n in range(len(GROUPS[i]) - 1):
            at = pr + n * (pr // 2)
            pay[i - 1, at : at + pr // 2, :] = piece[i, n + 1, keep, :] + far[i, n, keep, :]
        for copy in gathers[i - 1]:
            copy.start()
        bag[i - 1, side, core, chip, 0 : bag_rows[i - 1], :] = pay[i - 1, 0 : bag_rows[i - 1], :]

    def share(i):
        for copy in gathers[i - 1]:
            copy.wait_recv()
        for copy in bag_shares[i - 1]:
            copy.start()

    def unpack(i):
        for copy in bag_shares[i - 1]:
            copy.wait_recv()
        q[:, (i - 1) * r : i * r] = bag[i - 1, :, :, :, 0:pr, :].reshape(order, r)
        for n in range(len(GROUPS[i]) - 1):
            at = pr + n * (pr // 2)
            for t in range(2):
                s[ORDER[i, n], :, t] = bag[i - 1, t, :, :, at : at + pr // 2, :].reshape(
                    2 * chips, pr // 2, r
                )

    def swap(level, src, dst, n):
        return remote(src, dst, ex_sem.at[0, level, n], ex_sem.at[1, level, n], (far_gx[level], gy))

    def pass_on(level, ref, n):
        return remote(ref, ref, exs_sem.at[0, level, n], exs_sem.at[1, level, n], partner)

    mine = pl.ds(pl.multiple_of(core * hr, hr), hr)
    ex_g, ex_q, sh_g, sh_q = {}, {}, {}, {}
    for level, qs in ((1, q1), (2, q2)):
        to = pl.ds(pl.multiple_of(sides[level] * r + core * hr, hr), hr)
        come = pl.ds(pl.multiple_of((1 - sides[level]) * r + core * hr, hr), hr)
        ex_g[level] = swap(level, h.at[level - 1, 0, mine, :], g.at[level, to, :], 0)
        ex_q[level] = swap(level, qs.at[to, :], qs.at[to, :], 1)
        sh_g[level] = pass_on(level, g.at[level, come, :], 0)
        sh_q[level] = pass_on(level, qs.at[come, :], 1)
    ex_s = swap(1, s1.at[mine, :], tail, 2)
    sh_s = pass_on(1, s1.at[mine, :], 2)

    local(0)
    local(1)
    scatter(0)
    local(2)
    collect(0)
    g[0, pl.ds(row, pr), :] = piece[0, 0]
    for copy in g_gather:
        copy.start()
    scatter(1)
    local(3)
    scatter(2)
    collect(1)
    for copy in g_gather:
        copy.wait_recv()
    for copy in g_shares:
        copy.start()
    scatter(3)
    gather(1)
    collect(2)
    for copy in g_shares:
        copy.wait_recv()
    for copy in loads[4:]:
        copy.wait()

    eye = jnp.where(
        lax.broadcasted_iota(jnp.int32, (NB, NB), 0) == lax.broadcasted_iota(jnp.int32, (NB, NB), 1),
        1.0,
        0.0,
    )
    steps = order // NB

    def receive_q(level):
        ex_q[level].wait_recv()
        sh_q[level].start()

    def hook(level, j):
        if (level, j) == (0, 0):
            gather(2)
            collect(3)
        elif (level, j) == (0, 1):
            gather(3)
            share(1)
        elif (level, j) == (0, 2):
            share(2)
        elif (level, j) == (0, 3):
            share(3)
            unpack(1)
        elif (level, j) == (1, 2):
            receive_q(1)
            ex_s.wait()
            s1[mine, :] = s1[mine, :] + tail[...]
            sh_s.start()
        elif (level, j) == (2, 1):
            receive_q(2)

    def core_block(out, level, count):
        place = gx * 2 * chips + gy
        start = (place % (4 * chips << level)) * count
        at = pl.ds(pl.multiple_of((start // NB) * NB, NB), NB)
        krows[...] = dot3(split2(m[:, at]), split2(m[...]), TN)
        inner = start % NB
        if count % 8 == 0:
            out[...] = krows[pl.ds(pl.multiple_of(inner, 8), count), :]
        else:
            eight = krows[pl.ds(pl.multiple_of((inner // 8) * 8, 8), 8), :]
            out[...] = jnp.where(inner % 8 == 0, eight[:count], eight[count:])

    def own_of(level):
        return split2(m[:, pl.ds(pl.multiple_of(sides[level] * r, r), r)])

    def column(i):
        return split2(p[:, i * r : (i + 1) * r])

    def after(level):
        ms = split2(m[...])
        if level == 0:
            p[:, 0:r] = dot3(ms, split2(q[:, 0:r]), NN)
            p2 = column(0)
            h[0, 0] = s[0].reshape(r, r) - dot3(p2, p2, TN)
            ex_g[1].start()
            g[1, pl.ds(pl.multiple_of(sides[1] * r, r), r), :] = h[0, 0]
            unpack(2)
            unpack(3)
            p[:, r:] = dot3(ms, split2(q[:, r:]), NN)
            p1, pc = column(1), column(2)
            at = pl.ds(pl.multiple_of(sides[1] * r, r), r)
            q1[at, 0:r] = s[1].reshape(r, r) - dot3(p2, p1, TN)
            q1[at, r:] = s[2].reshape(r, r) - dot3(p2, pc, TN)
            ex_q[1].start()
            s1[:, 0:r] = s[3].reshape(r, r) - dot3(p1, p1, TN)
            s1[:, r:] = s[4].reshape(r, r) - dot3(p1, pc, TN)
            ex_s.start()
            ex_g[1].wait_recv()
            sh_g[1].start()
            v3[...] = dot3(own_of(0), split2(p[...]), TN)
            core_block(core3, 0, 16)
            sh_g[1].wait_recv()
        elif level == 1:
            sh_q[1].wait_recv()
            sh_s.wait_recv()
            p[:, 0:r] = dot3(ms, split2(q1[:, 0:r]), NN)
            p1 = column(0)
            h[1, 0] = s1[:, 0:r] - dot3(p1, p1, TN)
            ex_g[2].start()
            g[2, pl.ds(pl.multiple_of(sides[2] * r, r), r), :] = h[1, 0]
            p[:, r : 2 * r] = dot3(ms, split2(q1[:, r:]), NN)
            q2[pl.ds(pl.multiple_of(sides[2] * r, r), r), :] = s1[:, r:] - dot3(p1, column(1), TN)
            ex_q[2].start()
            ex_g[2].wait_recv()
            sh_g[2].start()
            v2[...] = dot3(own_of(1), split2(p[:, 0 : 2 * r]), TN)
            core_block(core2, 1, 8)
            sh_g[2].wait_recv()
        else:
            sh_q[2].wait_recv()
            x1 = dot3(own_of(2), split2(dot3(ms, split2(q2[...]), NN)), TN)
            t1 = split2(x1)
            x2 = v2[:, r:] - dot3(split2(v2[:, :r]), t1, NN)
            t2 = split2(x2)
            x3 = v3[:, 2 * r :] - dot3(split2(v3[:, :r]), t2, NN)
            x3 = x3 - dot3(split2(v3[:, r : 2 * r]), t1, NN)
            x[0:r, :] = x3
            x[r : 2 * r, :] = x2
            x[2 * r :, :] = x1
            core_block(core1, 2, 4)

    def one_level(level, carry):
        full = coupling[level]
        gl = jnp.concatenate(
            [dot6(g[level, :r, :], full[:r, :], NN), dot6(g[level, r:, :], full[r:, :], NN)], 0
        )
        for j in range(steps):
            o = j * NB
            c[o : o + NB, o:order] = dot6(full[:, o : o + NB], gl[:, o:], TN)
            c[o : o + NB, order:] = full[:, o : o + NB].T

        def step(j, carry):
            for jj in range(steps):

                @pl.when(j == jj)
                def _(o=jj * NB):
                    work[...] = c[o : o + NB, o : o + NB] + eye

            invert_factor(work)
            for jj in range(steps):

                @pl.when(j == jj)
                def _(jj=jj, o=jj * NB, t=jj * NB + NB):
                    out = dot6(work[...], c[o : o + NB, t:], NN)
                    m[o : o + NB, :] = out[:, order - t :]
                    for w in range(t, order, NB):
                        c[w : w + NB, w:] = c[w : w + NB, w:] - dot6(
                            out[:, w - t : w - t + NB], out[:, w - t :], TN
                        )

            for lv, jj in ((0, 0), (0, 1), (0, 2), (0, 3), (1, 2), (2, 1)):

                @pl.when((level == lv) & (j == jj))
                def _(lv=lv, jj=jj):
                    hook(lv, jj)

            return carry

        lax.fori_loop(0, steps, step, 0)
        for lv in range(3):

            @pl.when(level == lv)
            def _(lv=lv):
                after(lv)

        return carry

    lax.fori_loop(0, 3, one_level, 0)
    sends = [*nears, *g_gather, *g_shares, *across, ex_g[1], ex_g[2], ex_q[1], ex_q[2]]
    sends += [sh_g[1], sh_g[2], sh_q[1], sh_q[2], sh_s]
    for copies in (*scatters, *gathers, *bag_shares):
        sends += copies
    for copy in sends:
        copy.wait_send()


def mega(b3, b2, b1, rhs, leaf, cpl3, cpl2, cpl1):
    rows, r = b3.shape
    order = 2 * r
    chips = lax.axis_size("gy") // 2
    hr = r // 2
    pr = hr // chips
    most = max(len(y) for y in GROUPS)
    wide = pr + (pr // 2) * (most - 1)
    hbm = pl.BlockSpec(memory_space=pl.ANY)
    dma = pltpu.SemaphoreType.DMA

    def vmem(*shape):
        return pltpu.VMEM(shape, F32)

    return pl.pallas_call(
        lambda *refs: mega_kernel(chips, *refs),
        in_specs=[hbm] * 4 + [VMEM] + [hbm] * 3,
        out_specs=[VMEM] * 4,
        out_shape=[
            jax.ShapeDtypeStruct(shape, F32)
            for shape in ((3 * r, r), (16, order), (8, order), (4, order))
        ],
        scratch_shapes=[
            vmem(4, rows, r),
            pltpu.VMEM((4, rows, r), BF16),
            pltpu.VMEM((4, rows, r), BF16),
            vmem(4, most, r, r),
            vmem(4, most, hr, r),
            vmem(4, most, hr, r),
            vmem(4, chips - 1, most, pr, r),
            vmem(4, most, pr, r),
            vmem(4, most - 1, pr, r),
            vmem(3, wide, r),
            vmem(3, 2, 2, chips, wide, r),
            vmem(3, order, r),
            vmem(order, 3 * r),
            vmem(5, 2 * chips, 2, pr // 2, r),
            vmem(2, 1, r, r),
            vmem(order, 2 * r),
            vmem(r, 2 * r),
            vmem(hr, 2 * r),
            vmem(order, r),
            vmem(3, order, order),
            vmem(order, 2 * order),
            vmem(NB, NB),
            vmem(order, order),
            vmem(order, 3 * r),
            vmem(r, 3 * r),
            vmem(r, 2 * r),
            vmem(NB, order),
            dma((7,)),
            dma((2, 4)),
            dma((2, 4, chips - 1)),
            dma((2, 2 * chips - 1)),
            dma((2, 2)),
            dma((2, 4)),
            dma((2, 3, 2 * chips - 1)),
            dma((2, 3, 2)),
            dma((2, 3, 3)),
            dma((2, 3, 3)),
        ],
        compiler_params=pltpu.CompilerParams(
            collective_id=0, has_side_effects=True, vmem_limit_bytes=56 << 20
        ),
        name="mega",
    )(b3, b2, b1, rhs, leaf.reshape(rows // 128, 128), cpl3, cpl2, cpl1)


def apply_kernel(b3, b2, b1, rhs, leaf, x, k3, k2, k1, out, core3, core2, core1):
    r = b3.shape[1]

    @pl.when(pl.program_id(0) == 0)
    def _():
        core3[...] = k3[...]
        core2[...] = k2[...]
        core1[...] = k1[...]

    xs = split2(x[...])
    total = rhs[...]
    for i, b in enumerate((b3, b2, b1)):
        total = total - dot3(split2(b[...]), tuple(y[i * r : (i + 1) * r] for y in xs), NN)
    turned = leaf[0].T
    out[...] = total * jnp.concatenate([turned[:, u : u + 1] for u in range(leaf.shape[1])], 0)


def apply_update(b3, b2, b1, rhs, leaf, x, cores):
    rows, r = b3.shape
    tile = 512
    block = pl.BlockSpec((tile, r), lambda i: (i, 0))
    whole = [pl.BlockSpec(k.shape, lambda i: (0, 0)) for k in cores]
    return pl.pallas_call(
        apply_kernel,
        grid=(rows // tile,),
        in_specs=[block] * 4
        + [
            pl.BlockSpec((1, tile // 128, 128), lambda i: (i, 0, 0)),
            pl.BlockSpec(x.shape, lambda i: (0, 0)),
        ]
        + whole,
        out_specs=[block] + whole,
        out_shape=[jax.ShapeDtypeStruct(rhs.shape, F32)]
        + [jax.ShapeDtypeStruct(k.shape, F32) for k in cores],
        name="apply_update",
    )(b3, b2, b1, rhs, leaf.reshape(rows // tile, tile // 128, 128), x, *cores)


def per_device(basis3, basis2, basis1, leaf_inverse, rhs, coupling3, coupling2, coupling1):
    x, *cores = mega(
        basis3, basis2, basis1, rhs, leaf_inverse, coupling3, coupling2, coupling1
    )
    return tuple(apply_update(basis3, basis2, basis1, rhs, leaf_inverse, x, cores))


def solution(mesh):
    rows = P(("gx", "gy"), None)
    return jax.shard_map(
        per_device,
        mesh=mesh,
        in_specs=(rows, rows, rows, P(("gx", "gy")), rows, P(), P(), P()),
        out_specs=(rows, rows, rows, rows),
        check_vma=False,
    )
```

```python
import jax
import jax.numpy as jnp
from jax import lax
from jax.experimental import pallas as pl
from jax.experimental.pallas import tpu as pltpu
from jax.sharding import PartitionSpec as P

F32 = jnp.float32
BF16 = jnp.bfloat16
NN = ((1,), (0,))
TN = ((0,), (0,))
W = 32
NB = 128
VMEM = pl.BlockSpec(memory_space=pltpu.VMEM)


def dot6(a, b, dims):
    (i,), (j,) = dims
    left = jnp.concatenate([a[0], a[0], a[1], a[0], a[2], a[1]], i)
    right = jnp.concatenate([b[0], b[1], b[0], b[2], b[0], b[1]], j)
    return dot1(left, right, dims)


def dot1(a, b, dims):
    return lax.dot_general(a, b, (dims, ((), ())), preferred_element_type=F32)


def split2(x):
    hi = x.astype(BF16)
    return hi, (x - hi.astype(F32)).astype(BF16)


def split3(x):
    hi = x.astype(BF16)
    rest = x - hi.astype(F32)
    mid = rest.astype(BF16)
    return hi, mid, (rest - mid.astype(F32)).astype(BF16)


def dot3(a, b, dims):
    (i,), (j,) = dims
    left = jnp.concatenate([a[0], a[0], a[1]], i)
    right = jnp.concatenate([b[0], b[1], b[0]], j)
    return dot1(left, right, dims)


MESH = pl.DeviceIdType.MESH


def where_am_i():
    gx = lax.axis_index("gx")
    gy = lax.axis_index("gy")
    core = gy % 2
    return gx, gy, core, gy // 2, gy + 1 - 2 * core, gx + 1 - 2 * (gx % 2)


def greet(peers):
    barrier = pltpu.get_barrier_semaphore()
    for peer in peers:
        pl.semaphore_signal(barrier, inc=1, device_id=peer, device_id_type=MESH)


def all_met(peers):
    pl.semaphore_wait(pltpu.get_barrier_semaphore(), len(peers))


def group_peers(chips):
    gx, gy, core, chip, other, sib = where_am_i()
    own = [(gx, 2 * ((chip + d) % chips) + core) for d in range(1, chips)]
    far = [(sib, 2 * ((chip + d) % chips) + core) for d in range(chips)]
    return [(gx, other)] + own + far


def remote(src, dst, send, recv, peer):
    return pltpu.make_async_remote_copy(
        src_ref=src, dst_ref=dst, send_sem=send, recv_sem=recv, device_id=peer, device_id_type=MESH
    )


def invert_factor(work, spread):
    n = work.shape[0]
    parts = W // 8
    lane = lax.broadcasted_iota(jnp.int32, (8, n), 1)
    sub = lax.broadcasted_iota(jnp.int32, (8, n), 0)
    wide = lax.broadcasted_iota(jnp.int32, (W, n), 1)
    for s in range(n // W):
        o = s * W
        block = [work[o + 8 * h : o + 8 * h + 8, :] for h in range(parts)]
        for k in range(W):
            for h in range(k // 8, parts):
                spread[k, h] = jnp.broadcast_to(block[h][:, o + k : o + k + 1], (8, n))
        col = {(k, h): spread[k, h] for k in range(W) for h in range(k // 8, parts)}
        inside = (lane >= o) & (lane < o + W)
        x = [
            jnp.where(inside, jnp.where(lane - o == sub + 8 * h, 1.0, 0.0), block[h])
            for h in range(parts)
        ]
        for k in range(W):
            g, e = k // 8, k % 8
            d = col[k, g][e : e + 1]
            recip = 1.0 / d
            pivot_row = x[g][e : e + 1]
            for h in range(g, parts):
                m = col[k, h] * recip
                if h == g:
                    m = jnp.where(sub > e, m, 0.0)
                for j in range(k + 1, min(W, 8 * h + 8)):
                    col[j, h] = col[j, h] - m * col[k, j // 8][j % 8 : j % 8 + 1]
                x[h] = x[h] - m * pivot_row
            x[g] = jnp.where(sub == e, x[g] * lax.rsqrt(d), x[g])
        v = jnp.concatenate(x, 0)
        work[o : o + W, :] = jnp.where(wide < o + W, v, 0.0)
        t = o + W
        if t < n:
            v3 = split3(v)
            update = dot6(v3, v3, TN)
            below = lax.broadcasted_iota(jnp.int32, (n - t, n), 1)
            kept = jnp.where((below >= o) & (below < t), 0.0, work[t:, :])
            work[t:, :] = kept - update[t:, :]


GROUPS = (((0, 0),), ((0, 1), (1, 1)), ((0, 2), (1, 2), (2, 2)), ((0, 3), (1, 3), (2, 3)))
ORDER = {(1, 0): 0, (2, 0): 1, (2, 1): 3, (3, 0): 2, (3, 1): 4}
TILE = 512


def mega_kernel(
    chips, b3, b2, b1, rhs, leaf, cpl3, cpl2, cpl1, x, core3, core2, core1,
    raw, hi_t, lo_t, part, near, half, arrived, piece, far, pay, bag, g, q, s, h, q1, s1, tail, q2,
    coupling, turned, l_parts, lt_parts, c, work, spread, m, p, v3, v2, krows,
    load_sem, near_sem, rs_sem, ag_sem, share_sem, far_sem, bag_sem, bshare_sem, ex_sem, exs_sem,
):
    gx, gy, core, chip, other, sib = where_am_i()
    rows, r = b3.shape
    order = 2 * r
    tiles = rows // TILE
    per = TILE // leaf.shape[1]
    hr = r // 2
    pr = hr // chips
    sides = (gx % 2, (gx // 2) % 2, (gx // 4) % 2)
    far_gx = (sib, gx + 2 - 4 * sides[1], gx + 4 - 8 * sides[2])
    side = sides[0]
    partner = (gx, other)

    loads = [
        pltpu.make_async_copy(b, raw.at[i], load_sem.at[i]) for i, b in enumerate((b3, b2, b1, rhs))
    ]
    loads += [
        pltpu.make_async_copy(src.at[at], coupling.at[i], load_sem.at[4 + i])
        for i, (src, at) in enumerate(((cpl3, gx // 2), (cpl2, gx // 4), (cpl1, 0)))
    ]
    loads[0].start()
    peers = group_peers(chips)
    everyone = peers + [(far_gx[1], gy), (far_gx[2], gy)]
    greet(everyone)
    for copy in loads[1:]:
        copy.start()
    root = jnp.sqrt(leaf[...]).T

    nears = [
        remote(
            part.at[i, pl.ds(0, len(GROUPS[i])), pl.ds(pl.multiple_of((1 - core) * hr, hr), hr), :],
            near.at[i, pl.ds(0, len(GROUPS[i]))],
            near_sem.at[0, i], near_sem.at[1, i], partner,
        )
        for i in range(4)
    ]
    scatters = [
        [
            remote(
                half.at[
                    i, pl.ds(0, len(GROUPS[i])),
                    pl.ds(pl.multiple_of(((chip + d) % chips) * pr, pr), pr), :,
                ],
                arrived.at[i, d - 1, pl.ds(0, len(GROUPS[i]))],
                rs_sem.at[0, i, d - 1], rs_sem.at[1, i, d - 1], peers[d],
            )
            for d in range(1, chips)
        ]
        for i in range(4)
    ]
    row = pl.multiple_of(side * r + core * hr + chip * pr, pr)
    g_gather = [
        remote(
            piece.at[0, 0], g.at[0, pl.ds(row, pr), :], ag_sem.at[0, d], ag_sem.at[1, d], peer
        )
        for d, peer in enumerate(peers[1:])
    ]
    g_shares = []
    for t in range(2):
        at = g.at[0, pl.ds(pl.multiple_of(t * r + core * hr, hr), hr), :]
        g_shares.append(remote(at, at, share_sem.at[0, t], share_sem.at[1, t], partner))
    across = [
        remote(
            piece.at[i, pl.ds(1, len(GROUPS[i]) - 1)], far.at[i, pl.ds(0, len(GROUPS[i]) - 1)],
            far_sem.at[0, i], far_sem.at[1, i], (sib, gy),
        )
        for i in range(1, 4)
    ]
    bag_rows = [pr + (pr // 2) * (len(GROUPS[i]) - 1) for i in range(1, 4)]
    gathers = [
        [
            remote(
                pay.at[i, pl.ds(0, n), :], bag.at[i, side, core, chip, pl.ds(0, n), :],
                bag_sem.at[0, i, d], bag_sem.at[1, i, d], peer,
            )
            for d, peer in enumerate(peers[1:])
        ]
        for i, n in enumerate(bag_rows)
    ]
    bag_shares = [
        [
            remote(
                bag.at[i, t, core, :, pl.ds(0, n), :], bag.at[i, t, core, :, pl.ds(0, n), :],
                bshare_sem.at[0, i, t], bshare_sem.at[1, i, t], partner,
            )
            for t in range(2)
        ]
        for i, n in enumerate(bag_rows)
    ]

    def local(i):
        loads[i].wait()
        n = len(GROUPS[i])
        for t in range(tiles):
            at = slice(t * TILE, (t + 1) * TILE)
            scale = jnp.concatenate([root[:, t * per + u : t * per + u + 1] for u in range(per)], 0)
            upper, lower = split2(raw[i, at, :] * scale)
            if i < 3:
                hi_t[i, :, at] = upper.T
                lo_t[i, :, at] = lower.T
            left = tuple(
                jnp.concatenate([z[a, :, at] for a, b in GROUPS[i]], 0) for z in (hi_t, lo_t)
            )
            sums = dot3(left, (upper, lower), NN).reshape(n, r, r)
            part[i, 0:n] = sums if t == 0 else part[i, 0:n] + sums
        if i == 0:
            all_met(everyone)
        nears[i].start()

    def scatter(i):
        n = len(GROUPS[i])
        nears[i].wait_recv()
        half[i, 0:n] = part[i, 0:n, pl.ds(pl.multiple_of(core * hr, hr), hr), :] + near[i, 0:n]
        for copy in scatters[i]:
            copy.start()

    def collect(i):
        n = len(GROUPS[i])
        total = half[i, 0:n, pl.ds(pl.multiple_of(chip * pr, pr), pr), :]
        for d, copy in enumerate(scatters[i]):
            copy.wait_recv()
            total = total + arrived[i, d, 0:n]
        piece[i, 0:n] = total
        if i > 0:
            across[i - 1].start()

    def gather(i):
        across[i - 1].wait_recv()
        pay[i - 1, 0:pr, :] = piece[i, 0]
        keep = pl.ds(pl.multiple_of(side * (pr // 2), pr // 2), pr // 2)
        for n in range(len(GROUPS[i]) - 1):
            at = pr + n * (pr // 2)
            pay[i - 1, at : at + pr // 2, :] = piece[i, n + 1, keep, :] + far[i, n, keep, :]
        for copy in gathers[i - 1]:
            copy.start()
        bag[i - 1, side, core, chip, 0 : bag_rows[i - 1], :] = pay[i - 1, 0 : bag_rows[i - 1], :]

    def share(i):
        for copy in gathers[i - 1]:
            copy.wait_recv()
        for copy in bag_shares[i - 1]:
            copy.start()

    def unpack(i):
        for copy in bag_shares[i - 1]:
            copy.wait_recv()
        q[:, (i - 1) * r : i * r] = bag[i - 1, :, :, :, 0:pr, :].reshape(order, r)
        for n in range(len(GROUPS[i]) - 1):
            at = pr + n * (pr // 2)
            for t in range(2):
                s[ORDER[i, n], :, t] = bag[i - 1, t, :, :, at : at + pr // 2, :].reshape(
                    2 * chips, pr // 2, r
                )

    def swap(level, src, dst, n):
        return remote(src, dst, ex_sem.at[0, level, n], ex_sem.at[1, level, n], (far_gx[level], gy))

    def pass_on(level, ref, n):
        return remote(ref, ref, exs_sem.at[0, level, n], exs_sem.at[1, level, n], partner)

    mine = pl.ds(pl.multiple_of(core * hr, hr), hr)
    ex_g, ex_q, sh_g, sh_q = {}, {}, {}, {}
    for level, qs in ((1, q1), (2, q2)):
        to = pl.ds(pl.multiple_of(sides[level] * r + core * hr, hr), hr)
        come = pl.ds(pl.multiple_of((1 - sides[level]) * r + core * hr, hr), hr)
        ex_g[level] = swap(level, h.at[level - 1, 0, mine, :], g.at[level, to, :], 0)
        ex_q[level] = swap(level, qs.at[to, :], qs.at[to, :], 1)
        sh_g[level] = pass_on(level, g.at[level, come, :], 0)
        sh_q[level] = pass_on(level, qs.at[come, :], 1)
    ex_s = swap(1, s1.at[mine, :], tail, 2)
    sh_s = pass_on(1, s1.at[mine, :], 2)

    def prepare(level):
        loads[4 + level].wait()
        across_rows = coupling[level].T
        turned[level] = across_rows
        for n, (y, z) in enumerate(zip(split3(coupling[level]), split3(across_rows))):
            l_parts[level, n] = y
            lt_parts[level, n] = z

    local(0)
    local(1)
    scatter(0)
    local(2)
    collect(0)
    g[0, pl.ds(row, pr), :] = piece[0, 0]
    for copy in g_gather:
        copy.start()
    scatter(1)
    local(3)
    scatter(2)
    collect(1)
    for copy in g_gather:
        copy.wait_recv()
    for copy in g_shares:
        copy.start()
    scatter(3)
    gather(1)
    collect(2)
    prepare(0)
    for copy in g_shares:
        copy.wait_recv()

    eye = jnp.where(
        lax.broadcasted_iota(jnp.int32, (NB, NB), 0) == lax.broadcasted_iota(jnp.int32, (NB, NB), 1),
        1.0,
        0.0,
    )
    steps = order // NB

    def receive_q(level):
        ex_q[level].wait_recv()
        sh_q[level].start()

    def hook(level, j):
        if (level, j) == (0, 0):
            gather(2)
            collect(3)
        elif (level, j) == (0, 1):
            gather(3)
            share(1)
        elif (level, j) == (0, 2):
            share(2)
        elif (level, j) == (0, 3):
            share(3)
            unpack(1)
        elif (level, j) == (1, 2):
            receive_q(1)
            ex_s.wait()
            s1[mine, :] = s1[mine, :] + tail[...]
            sh_s.start()
        elif (level, j) == (2, 1):
            receive_q(2)

    def core_block(out, level, count):
        place = gx * 2 * chips + gy
        start = (place % (4 * chips << level)) * count
        at = pl.ds(pl.multiple_of((start // NB) * NB, NB), NB)
        krows[...] = dot3(split2(m[:, at]), split2(m[...]), TN)
        inner = start % NB
        if count % 8 == 0:
            out[...] = krows[pl.ds(pl.multiple_of(inner, 8), count), :]
        else:
            eight = krows[pl.ds(pl.multiple_of((inner // 8) * 8, 8), 8), :]
            out[...] = jnp.where(inner % 8 == 0, eight[:count], eight[count:])

    def own_of(level):
        return split2(m[:, pl.ds(pl.multiple_of(sides[level] * r, r), r)])

    def column(i):
        return split2(p[:, i * r : (i + 1) * r])

    def after(level):
        ms = split2(m[...])
        if level == 0:
            p[:, 0:r] = dot3(ms, split2(q[:, 0:r]), NN)
            p2 = column(0)
            h[0, 0] = s[0].reshape(r, r) - dot3(p2, p2, TN)
            ex_g[1].start()
            g[1, pl.ds(pl.multiple_of(sides[1] * r, r), r), :] = h[0, 0]
            unpack(2)
            unpack(3)
            p[:, r:] = dot3(ms, split2(q[:, r:]), NN)
            p1, pc = column(1), column(2)
            at = pl.ds(pl.multiple_of(sides[1] * r, r), r)
            q1[at, 0:r] = s[1].reshape(r, r) - dot3(p2, p1, TN)
            q1[at, r:] = s[2].reshape(r, r) - dot3(p2, pc, TN)
            ex_q[1].start()
            s1[:, 0:r] = s[3].reshape(r, r) - dot3(p1, p1, TN)
            s1[:, r:] = s[4].reshape(r, r) - dot3(p1, pc, TN)
            ex_s.start()
            prepare(1)
            ex_g[1].wait_recv()
            sh_g[1].start()
            v3[...] = dot3(own_of(0), split2(p[...]), TN)
            core_block(core3, 0, 16)
            sh_g[1].wait_recv()
        elif level == 1:
            sh_q[1].wait_recv()
            sh_s.wait_recv()
            p[:, 0:r] = dot3(ms, split2(q1[:, 0:r]), NN)
            p1 = column(0)
            h[1, 0] = s1[:, 0:r] - dot3(p1, p1, TN)
            ex_g[2].start()
            g[2, pl.ds(pl.multiple_of(sides[2] * r, r), r), :] = h[1, 0]
            p[:, r : 2 * r] = dot3(ms, split2(q1[:, r:]), NN)
            q2[pl.ds(pl.multiple_of(sides[2] * r, r), r), :] = s1[:, r:] - dot3(p1, column(1), TN)
            ex_q[2].start()
            prepare(2)
            ex_g[2].wait_recv()
            sh_g[2].start()
            v2[...] = dot3(own_of(1), split2(p[:, 0 : 2 * r]), TN)
            core_block(core2, 1, 8)
            sh_g[2].wait_recv()
        else:
            sh_q[2].wait_recv()
            x1 = dot3(own_of(2), split2(dot3(ms, split2(q2[...]), NN)), TN)
            t1 = split2(x1)
            x2 = v2[:, r:] - dot3(split2(v2[:, :r]), t1, NN)
            t2 = split2(x2)
            x3 = v3[:, 2 * r :] - dot3(split2(v3[:, :r]), t2, NN)
            x3 = x3 - dot3(split2(v3[:, r : 2 * r]), t1, NN)
            x[0:r, :] = x3
            x[r : 2 * r, :] = x2
            x[2 * r :, :] = x1
            core_block(core1, 2, 4)

    def one_level(level, carry):
        l3 = [l_parts[level, n] for n in range(3)]
        lt3 = [lt_parts[level, n] for n in range(3)]
        g3 = split3(g[level])
        gl = jnp.concatenate(
            [
                dot6([y[at] for y in g3], [y[at] for y in l3], NN)
                for at in (slice(0, r), slice(r, order))
            ],
            0,
        )
        gl3 = split3(gl)
        for o in range(0, order, NB):
            at = slice(o, o + NB)
            c[at, o:order] = dot6([y[at] for y in lt3], [y[:, o:] for y in gl3], NN)
            c[at, order:] = turned[level, at, :]
        work[...] = c[0:NB, 0:NB] + eye
        behind = None
        for j in range(steps):
            o = j * NB
            t = o + NB
            u = t + NB
            if behind is not None:
                behind()
            invert_factor(work, spread)
            inverse = split3(work[...])
            if t < order:
                near_row = split3(dot6(inverse, split3(c[o:t, t:u]), NN))
                work[...] = c[t:u, t:u] - dot6(near_row, near_row, TN) + eye

                def behind(o=o, t=t, u=u, inverse=inverse, near_row=near_row):
                    out = dot6(inverse, split3(c[o:t, u:]), NN)
                    m[o:t, :] = out[:, order - u :]
                    out3 = split3(out)
                    c[t:u, u:] = c[t:u, u:] - dot6(near_row, out3, TN)
                    for w in range(u, order, NB):
                        a = w - u
                        c[w : w + NB, w:] = c[w : w + NB, w:] - dot6(
                            [y[:, a : a + NB] for y in out3], [y[:, a:] for y in out3], TN
                        )

            else:
                m[o:t, :] = dot6(inverse, split3(c[o:t, order:]), NN)
            for lv, jj in ((0, 0), (0, 1), (0, 2), (0, 3), (1, 2), (2, 1)):
                if jj == j:

                    @pl.when(level == lv)
                    def _(lv=lv, jj=jj):
                        hook(lv, jj)

        for lv in range(3):

            @pl.when(level == lv)
            def _(lv=lv):
                after(lv)

        return carry

    lax.fori_loop(0, 3, one_level, 0)
    sends = [*nears, *g_gather, *g_shares, *across, ex_g[1], ex_g[2], ex_q[1], ex_q[2]]
    sends += [sh_g[1], sh_g[2], sh_q[1], sh_q[2], sh_s]
    for copies in (*scatters, *gathers, *bag_shares):
        sends += copies
    for copy in sends:
        copy.wait_send()


def mega(b3, b2, b1, rhs, leaf, cpl3, cpl2, cpl1):
    rows, r = b3.shape
    order = 2 * r
    chips = lax.axis_size("gy") // 2
    hr = r // 2
    pr = hr // chips
    most = max(len(y) for y in GROUPS)
    wide = pr + (pr // 2) * (most - 1)
    hbm = pl.BlockSpec(memory_space=pl.ANY)
    dma = pltpu.SemaphoreType.DMA

    def vmem(*shape):
        return pltpu.VMEM(shape, F32)

    return pl.pallas_call(
        lambda *refs: mega_kernel(chips, *refs),
        in_specs=[hbm] * 4 + [VMEM] + [hbm] * 3,
        out_specs=[VMEM] * 4,
        out_shape=[
            jax.ShapeDtypeStruct(shape, F32)
            for shape in ((3 * r, r), (16, order), (8, order), (4, order))
        ],
        scratch_shapes=[
            vmem(4, rows, r),
            pltpu.VMEM((3, r, rows), BF16),
            pltpu.VMEM((3, r, rows), BF16),
            vmem(4, most, r, r),
            vmem(4, most, hr, r),
            vmem(4, most, hr, r),
            vmem(4, chips - 1, most, pr, r),
            vmem(4, most, pr, r),
            vmem(4, most - 1, pr, r),
            vmem(3, wide, r),
            vmem(3, 2, 2, chips, wide, r),
            vmem(3, order, r),
            vmem(order, 3 * r),
            vmem(5, 2 * chips, 2, pr // 2, r),
            vmem(2, 1, r, r),
            vmem(order, 2 * r),
            vmem(r, 2 * r),
            vmem(hr, 2 * r),
            vmem(order, r),
            vmem(3, order, order),
            vmem(3, order, order),
            pltpu.VMEM((3, 3, order, order), BF16),
            pltpu.VMEM((3, 3, order, order), BF16),
            vmem(order, 2 * order),
            vmem(NB, NB),
            vmem(W, W // 8, 8, NB),
            vmem(order, order),
            vmem(order, 3 * r),
            vmem(r, 3 * r),
            vmem(r, 2 * r),
            vmem(NB, order),
            dma((7,)),
            dma((2, 4)),
            dma((2, 4, chips - 1)),
            dma((2, 2 * chips - 1)),
            dma((2, 2)),
            dma((2, 4)),
            dma((2, 3, 2 * chips - 1)),
            dma((2, 3, 2)),
            dma((2, 3, 3)),
            dma((2, 3, 3)),
        ],
        compiler_params=pltpu.CompilerParams(
            collective_id=0, has_side_effects=True, vmem_limit_bytes=60 << 20
        ),
        name="mega",
    )(b3, b2, b1, rhs, leaf.reshape(rows // 128, 128), cpl3, cpl2, cpl1)


def apply_kernel(b3, b2, b1, rhs, leaf, x, k3, k2, k1, out, core3, core2, core1):
    r = b3.shape[1]

    @pl.when(pl.program_id(0) == 0)
    def _():
        core3[...] = k3[...]
        core2[...] = k2[...]
        core1[...] = k1[...]

    xs = split2(x[...])
    total = rhs[...]
    for i, b in enumerate((b3, b2, b1)):
        total = total - dot3(split2(b[...]), tuple(y[i * r : (i + 1) * r] for y in xs), NN)
    turned = leaf[0].T
    out[...] = total * jnp.concatenate([turned[:, u : u + 1] for u in range(leaf.shape[1])], 0)


def apply_update(b3, b2, b1, rhs, leaf, x, cores):
    rows, r = b3.shape
    tile = 512
    block = pl.BlockSpec((tile, r), lambda i: (i, 0))
    whole = [pl.BlockSpec(k.shape, lambda i: (0, 0)) for k in cores]
    return pl.pallas_call(
        apply_kernel,
        grid=(rows // tile,),
        in_specs=[block] * 4
        + [
            pl.BlockSpec((1, tile // 128, 128), lambda i: (i, 0, 0)),
            pl.BlockSpec(x.shape, lambda i: (0, 0)),
        ]
        + whole,
        out_specs=[block] + whole,
        out_shape=[jax.ShapeDtypeStruct(rhs.shape, F32)]
        + [jax.ShapeDtypeStruct(k.shape, F32) for k in cores],
        name="apply_update",
    )(b3, b2, b1, rhs, leaf.reshape(rows // tile, tile // 128, 128), x, *cores)


def per_device(basis3, basis2, basis1, leaf_inverse, rhs, coupling3, coupling2, coupling1):
    x, *cores = mega(
        basis3, basis2, basis1, rhs, leaf_inverse, coupling3, coupling2, coupling1
    )
    return tuple(apply_update(basis3, basis2, basis1, rhs, leaf_inverse, x, cores))


def solution(mesh):
    rows = P(("gx", "gy"), None)
    return jax.shard_map(
        per_device,
        mesh=mesh,
        in_specs=(rows, rows, rows, P(("gx", "gy")), rows, P(), P(), P()),
        out_specs=(rows, rows, rows, rows),
        check_vma=False,
    )
```

```python
import jax
import jax.numpy as jnp
from jax import lax
from jax.experimental import pallas as pl
from jax.experimental.pallas import tpu as pltpu
from jax.sharding import PartitionSpec as P

F32 = jnp.float32
BF16 = jnp.bfloat16
NN = ((1,), (0,))
TN = ((0,), (0,))
W = 32
NB = 128
VMEM = pl.BlockSpec(memory_space=pltpu.VMEM)


def dot6(a, b, dims):
    (i,), (j,) = dims
    left = jnp.concatenate([a[0], a[0], a[1], a[0], a[2], a[1]], i)
    right = jnp.concatenate([b[0], b[1], b[0], b[2], b[0], b[1]], j)
    return dot1(left, right, dims)


def dot1(a, b, dims):
    return lax.dot_general(a, b, (dims, ((), ())), preferred_element_type=F32)


def split2(x):
    hi = x.astype(BF16)
    return hi, (x - hi.astype(F32)).astype(BF16)


def split3(x):
    hi = x.astype(BF16)
    rest = x - hi.astype(F32)
    mid = rest.astype(BF16)
    return hi, mid, (rest - mid.astype(F32)).astype(BF16)


def dot3(a, b, dims):
    (i,), (j,) = dims
    left = jnp.concatenate([a[0], a[0], a[1]], i)
    right = jnp.concatenate([b[0], b[1], b[0]], j)
    return dot1(left, right, dims)


MESH = pl.DeviceIdType.MESH


def where_am_i():
    gx = lax.axis_index("gx")
    gy = lax.axis_index("gy")
    core = gy % 2
    return gx, gy, core, gy // 2, gy + 1 - 2 * core, gx + 1 - 2 * (gx % 2)


def greet(peers):
    barrier = pltpu.get_barrier_semaphore()
    for peer in peers:
        pl.semaphore_signal(barrier, inc=1, device_id=peer, device_id_type=MESH)


def all_met(peers):
    pl.semaphore_wait(pltpu.get_barrier_semaphore(), len(peers))


def group_peers(chips):
    gx, gy, core, chip, other, sib = where_am_i()
    own = [(gx, 2 * ((chip + d) % chips) + core) for d in range(1, chips)]
    far = [(sib, 2 * ((chip + d) % chips) + core) for d in range(chips)]
    return [(gx, other)] + own + far


def remote(src, dst, send, recv, peer):
    return pltpu.make_async_remote_copy(
        src_ref=src, dst_ref=dst, send_sem=send, recv_sem=recv, device_id=peer, device_id_type=MESH
    )


def invert_factor(work, spread):
    n = work.shape[0]
    parts = W // 8
    lane = lax.broadcasted_iota(jnp.int32, (8, n), 1)
    sub = lax.broadcasted_iota(jnp.int32, (8, n), 0)
    wide = lax.broadcasted_iota(jnp.int32, (W, n), 1)
    for s in range(n // W):
        o = s * W
        block = [work[o + 8 * h : o + 8 * h + 8, :] for h in range(parts)]
        for k in range(W):
            for h in range(k // 8, parts):
                spread[k, h] = jnp.broadcast_to(block[h][:, o + k : o + k + 1], (8, n))
        col = {(k, h): spread[k, h] for k in range(W) for h in range(k // 8, parts)}
        inside = (lane >= o) & (lane < o + W)
        x = [
            jnp.where(inside, jnp.where(lane - o == sub + 8 * h, 1.0, 0.0), block[h])
            for h in range(parts)
        ]
        for k in range(W):
            g, e = k // 8, k % 8
            d = col[k, g][e : e + 1]
            recip = 1.0 / d
            pivot_row = x[g][e : e + 1]
            for h in range(g, parts):
                m = col[k, h] * recip
                if h == g:
                    m = jnp.where(sub > e, m, 0.0)
                for j in range(k + 1, min(W, 8 * h + 8)):
                    col[j, h] = col[j, h] - m * col[k, j // 8][j % 8 : j % 8 + 1]
                x[h] = x[h] - m * pivot_row
            x[g] = jnp.where(sub == e, x[g] * lax.rsqrt(d), x[g])
        v = jnp.concatenate(x, 0)
        work[o : o + W, :] = jnp.where(wide < o + W, v, 0.0)
        t = o + W
        if t < n:
            v3 = split3(v)
            update = dot6(v3, v3, TN)
            below = lax.broadcasted_iota(jnp.int32, (n - t, n), 1)
            kept = jnp.where((below >= o) & (below < t), 0.0, work[t:, :])
            work[t:, :] = kept - update[t:, :]


GROUPS = (((0, 0),), ((0, 1), (1, 1)), ((0, 2), (1, 2), (2, 2)), ((0, 3), (1, 3), (2, 3)))
ORDER = {(2, 0): 0, (3, 0): 1, (2, 1): 2, (3, 1): 3}
TILE = 512


def mega_kernel(
    chips, b3, b2, b1, rhs, leaf, cpl3, cpl2, cpl1, x, core3, core2, core1,
    raw, hi_t, lo_t, part, near, half, arrived, piece, far, pay, bag, g, q, s, own_s, h, q1, rows_q1, rows_q1_tail, s1, tail, tail_in, q2, rows_q2, strip,
    coupling, turned, l_parts, lt_parts, c, work, spread, m, p, v3, v2, krows,
    load_sem, near_sem, rs_sem, ag_sem, share_sem, far_sem, bag_sem, bshare_sem, ex_sem, exs_sem, wide_sem, s1_sem, tail_sem, last_sem,
):
    gx, gy, core, chip, other, sib = where_am_i()
    rows, r = b3.shape
    order = 2 * r
    tiles = rows // TILE
    per = TILE // leaf.shape[1]
    hr = r // 2
    pr = hr // chips
    sides = (gx % 2, (gx // 2) % 2, (gx // 4) % 2)
    far_gx = (sib, gx + 2 - 4 * sides[1], gx + 4 - 8 * sides[2])
    side = sides[0]
    partner = (gx, other)

    loads = [
        pltpu.make_async_copy(b, raw.at[i], load_sem.at[i]) for i, b in enumerate((b3, b2, b1, rhs))
    ]
    loads += [
        pltpu.make_async_copy(src.at[at], coupling.at[i], load_sem.at[4 + i])
        for i, (src, at) in enumerate(((cpl3, gx // 2), (cpl2, gx // 4), (cpl1, 0)))
    ]
    loads[0].start()
    peers = group_peers(chips)
    beyond = {}
    for level in (1, 2):
        beyond[level] = [
            (base, 2 * ((chip + d) % chips) + core)
            for base in (far_gx[level], far_gx[level] + 1 - 2 * (gx % 2))
            for d in range(chips)
        ]
    everyone = peers + beyond[1] + beyond[2]
    greet(everyone)
    for copy in loads[1:]:
        copy.start()
    root = jnp.sqrt(leaf[...]).T

    nears = [
        remote(
            part.at[i, pl.ds(0, len(GROUPS[i])), pl.ds(pl.multiple_of((1 - core) * hr, hr), hr), :],
            near.at[i, pl.ds(0, len(GROUPS[i]))],
            near_sem.at[0, i], near_sem.at[1, i], partner,
        )
        for i in range(4)
    ]
    scatters = [
        [
            remote(
                half.at[
                    i, pl.ds(0, len(GROUPS[i])),
                    pl.ds(pl.multiple_of(((chip + d) % chips) * pr, pr), pr), :,
                ],
                arrived.at[i, d - 1, pl.ds(0, len(GROUPS[i]))],
                rs_sem.at[0, i, d - 1], rs_sem.at[1, i, d - 1], peers[d],
            )
            for d in range(1, chips)
        ]
        for i in range(4)
    ]
    row = pl.multiple_of(side * r + core * hr + chip * pr, pr)
    g_gather = [
        remote(
            piece.at[0, 0], g.at[0, pl.ds(row, pr), :], ag_sem.at[0, d], ag_sem.at[1, d], peer
        )
        for d, peer in enumerate(peers[1:])
    ]
    g_shares = []
    for t in range(2):
        at = g.at[0, pl.ds(pl.multiple_of(t * r + core * hr, hr), hr), :]
        g_shares.append(remote(at, at, share_sem.at[0, t], share_sem.at[1, t], partner))
    across = [
        remote(
            piece.at[i, pl.ds(1, len(GROUPS[i]) - 1)], far.at[i, pl.ds(0, len(GROUPS[i]) - 1)],
            far_sem.at[0, i], far_sem.at[1, i], (sib, gy),
        )
        for i in range(1, 4)
    ]
    bag_rows = [pr + pr // 2, pr, pr]
    gathers = [
        [
            remote(
                pay.at[i, pl.ds(0, n), :], bag.at[i, side, core, chip, pl.ds(0, n), :],
                bag_sem.at[0, i, d], bag_sem.at[1, i, d], peer,
            )
            for d, peer in enumerate(peers[1:])
        ]
        for i, n in enumerate(bag_rows)
    ]
    bag_shares = [
        [
            remote(
                bag.at[i, t, core, :, pl.ds(0, n), :], bag.at[i, t, core, :, pl.ds(0, n), :],
                bshare_sem.at[0, i, t], bshare_sem.at[1, i, t], partner,
            )
            for t in range(2)
        ]
        for i, n in enumerate(bag_rows)
    ]

    def local(i):
        loads[i].wait()
        n = len(GROUPS[i])
        for t in range(tiles):
            at = slice(t * TILE, (t + 1) * TILE)
            scale = jnp.concatenate([root[:, t * per + u : t * per + u + 1] for u in range(per)], 0)
            upper, lower = split2(raw[i, at, :] * scale)
            if i < 3:
                hi_t[i, :, at] = upper.T
                lo_t[i, :, at] = lower.T
            left = tuple(
                jnp.concatenate([z[a, :, at] for a, b in GROUPS[i]], 0) for z in (hi_t, lo_t)
            )
            sums = dot3(left, (upper, lower), NN).reshape(n, r, r)
            part[i, 0:n] = sums if t == 0 else part[i, 0:n] + sums
        if i == 0:
            all_met(everyone)
        nears[i].start()

    def scatter(i):
        n = len(GROUPS[i])
        nears[i].wait_recv()
        half[i, 0:n] = part[i, 0:n, pl.ds(pl.multiple_of(core * hr, hr), hr), :] + near[i, 0:n]
        for copy in scatters[i]:
            copy.start()

    def collect(i):
        n = len(GROUPS[i])
        total = half[i, 0:n, pl.ds(pl.multiple_of(chip * pr, pr), pr), :]
        for d, copy in enumerate(scatters[i]):
            copy.wait_recv()
            total = total + arrived[i, d, 0:n]
        piece[i, 0:n] = total
        if i > 0:
            across[i - 1].start()

    keep = pl.ds(pl.multiple_of(side * (pr // 2), pr // 2), pr // 2)

    def gather(i):
        pay[i - 1, 0:pr, :] = piece[i, 0]
        if i == 1:
            across[0].wait_recv()
            pay[0, pr:, :] = piece[1, 1, keep, :] + far[1, 0, keep, :]
        for copy in gathers[i - 1]:
            copy.start()
        bag[i - 1, side, core, chip, 0 : bag_rows[i - 1], :] = pay[i - 1, 0 : bag_rows[i - 1], :]

    def keep_sums(i):
        across[i - 1].wait_recv()
        for n in range(2):
            own_s[:, ORDER[i, n] * r : (ORDER[i, n] + 1) * r] = (
                piece[i, n + 1, keep, :] + far[i, n, keep, :]
            )

    def share(i):
        for copy in gathers[i - 1]:
            copy.wait_recv()
        for copy in bag_shares[i - 1]:
            copy.start()

    def unpack(i):
        for copy in bag_shares[i - 1]:
            copy.wait_recv()
        q[:, (i - 1) * r : i * r] = bag[i - 1, :, :, :, 0:pr, :].reshape(order, r)
        if i == 1:
            for t in range(2):
                s[:, t] = bag[0, t, :, :, pr:, :].reshape(2 * chips, pr // 2, r)

    def swap(level, src, dst, n):
        return remote(src, dst, ex_sem.at[0, level, n], ex_sem.at[1, level, n], (far_gx[level], gy))

    def pass_on(level, ref, n):
        return remote(ref, ref, exs_sem.at[0, level, n], exs_sem.at[1, level, n], partner)

    mine = pl.ds(pl.multiple_of(core * hr, hr), hr)
    ex_g, sh_g, sh_q = {}, {}, {}
    for level, qs in ((1, q1), (2, q2)):
        to = pl.ds(pl.multiple_of(sides[level] * r + core * hr, hr), hr)
        come = pl.ds(pl.multiple_of((1 - sides[level]) * r + core * hr, hr), hr)
        ex_g[level] = swap(level, h.at[level - 1, mine, :], g.at[level, to, :], 0)
        sh_g[level] = pass_on(level, g.at[level, come, :], 0)
        sh_q[level] = [pass_on(level, qs.at[at, :], 1 + n) for n, at in enumerate((to, come))]
    sh_s = pass_on(1, s1.at[mine, :], 3)
    low = pl.multiple_of(chip * pr + side * (pr // 2), pr // 2)
    eight = pl.ds(low, pr // 2)
    s1_at = pl.ds(pl.multiple_of(core * hr + low, pr // 2), pr // 2)
    q_at = {
        level: pl.ds(pl.multiple_of(sides[level] * r + core * hr + low, pr // 2), pr // 2)
        for level in (1, 2)
    }
    wide_q1 = [
        remote(rows_q1, q1.at[q_at[1], :], wide_sem.at[0, d], wide_sem.at[1, d], peer)
        for d, peer in enumerate(peers[1:] + beyond[1])
    ]
    wide_q2 = [
        remote(rows_q2, q2.at[q_at[2], :], last_sem.at[0, d], last_sem.at[1, d], peer)
        for d, peer in enumerate(peers[1:] + beyond[2])
    ]
    s1_gather = [
        remote(tail.at[:, pl.ds(0, r)], s1.at[s1_at, :], s1_sem.at[0, d], s1_sem.at[1, d], peer)
        for d, peer in enumerate(peers[1:])
    ]
    tail_swap = remote(
        rows_q1_tail, tail_in, tail_sem.at[0], tail_sem.at[1], (far_gx[1], gy)
    )

    def prepare(level):
        loads[4 + level].wait()
        across_rows = coupling[level].T
        turned[level] = across_rows
        for n, (y, z) in enumerate(zip(split3(coupling[level]), split3(across_rows))):
            l_parts[level, n] = y
            lt_parts[level, n] = z

    local(0)
    local(1)
    scatter(0)
    local(2)
    collect(0)
    g[0, pl.ds(row, pr), :] = piece[0, 0]
    for copy in g_gather:
        copy.start()
    scatter(1)
    local(3)
    scatter(2)
    collect(1)
    for copy in g_gather:
        copy.wait_recv()
    for copy in g_shares:
        copy.start()
    scatter(3)
    gather(1)
    collect(2)
    gather(2)
    prepare(0)
    for copy in g_shares:
        copy.wait_recv()

    eye = jnp.where(
        lax.broadcasted_iota(jnp.int32, (NB, NB), 0) == lax.broadcasted_iota(jnp.int32, (NB, NB), 1),
        1.0,
        0.0,
    )
    steps = order // NB

    def hook(level, j):
        if (level, j) == (0, 0):
            collect(3)
            gather(3)
            keep_sums(2)
        elif (level, j) == (0, 1):
            keep_sums(3)
            share(1)
        elif (level, j) == (0, 2):
            share(2)
        elif (level, j) == (0, 3):
            share(3)
            unpack(1)
        elif (level, j) == (1, 0):
            tail_swap.wait_recv()
            tail[...] = rows_q1_tail[...] + tail_in[...]
            for copy in s1_gather:
                copy.start()
            s1[s1_at, :] = tail[:, 0:r]
        elif (level, j) == (1, 1):
            for copy in wide_q1:
                copy.wait_recv()
            for copy in sh_q[1]:
                copy.start()
        elif (level, j) == (1, 2):
            for copy in s1_gather:
                copy.wait_recv()
            sh_s.start()
        elif (level, j) == (2, 1):
            for copy in wide_q2:
                copy.wait_recv()
            for copy in sh_q[2]:
                copy.start()

    def core_block(out, level, count):
        place = gx * 2 * chips + gy
        start = (place % (4 * chips << level)) * count
        at = pl.ds(pl.multiple_of((start // NB) * NB, NB), NB)
        krows[...] = dot3(split2(m[:, at]), split2(m[...]), TN)
        inner = start % NB
        if count % 8 == 0:
            out[...] = krows[pl.ds(pl.multiple_of(inner, 8), count), :]
        else:
            eight = krows[pl.ds(pl.multiple_of((inner // 8) * 8, 8), 8), :]
            out[...] = jnp.where(inner % 8 == 0, eight[:count], eight[count:])

    def own_of(level):
        return split2(m[:, pl.ds(pl.multiple_of(sides[level] * r, r), r)])

    def column(i):
        return split2(p[:, i * r : (i + 1) * r])

    def strip_of(i, right, count):
        left = split2(p[:, pl.ds(pl.multiple_of(i * r + core * hr, hr), hr)])
        strip[:, 0:count] = dot3(left, right, TN)

    def after(level):
        ms = split2(m[...])
        if level == 0:
            p[:, 0:r] = dot3(ms, split2(q[:, 0:r]), NN)
            p2 = column(0)
            h[0] = s[...].reshape(r, r) - dot3(p2, p2, TN)
            ex_g[1].start()
            g[1, pl.ds(pl.multiple_of(sides[1] * r, r), r), :] = h[0]
            unpack(2)
            unpack(3)
            p[:, r:] = dot3(ms, split2(q[:, r:]), NN)
            right = split2(p[:, r:])
            strip_of(1, right, 2 * r)
            rows_q1_tail[...] = own_s[:, 2 * r :] - strip[eight, :]
            tail_swap.start()
            strip_of(0, right, 2 * r)
            rows_q1[...] = own_s[:, 0 : 2 * r] - strip[eight, :]
            for copy in wide_q1:
                copy.start()
            q1[q_at[1], :] = rows_q1[...]
            prepare(1)
            ex_g[1].wait_recv()
            sh_g[1].start()
            v3[...] = dot3(own_of(0), split2(p[...]), TN)
            core_block(core3, 0, 16)
            sh_g[1].wait_recv()
        elif level == 1:
            for copy in (*sh_q[1], sh_s):
                copy.wait_recv()
            p[:, 0:r] = dot3(ms, split2(q1[:, 0:r]), NN)
            p1 = column(0)
            h[1] = s1[...] - dot3(p1, p1, TN)
            ex_g[2].start()
            g[2, pl.ds(pl.multiple_of(sides[2] * r, r), r), :] = h[1]
            p[:, r : 2 * r] = dot3(ms, split2(q1[:, r:]), NN)
            strip_of(0, column(1), r)
            rows_q2[...] = tail[:, r:] - strip[eight, 0:r]
            for copy in wide_q2:
                copy.start()
            q2[q_at[2], :] = rows_q2[...]
            prepare(2)
            ex_g[2].wait_recv()
            sh_g[2].start()
            v2[...] = dot3(own_of(1), split2(p[:, 0 : 2 * r]), TN)
            core_block(core2, 1, 8)
            sh_g[2].wait_recv()
        else:
            for copy in sh_q[2]:
                copy.wait_recv()
            x1 = dot3(own_of(2), split2(dot3(ms, split2(q2[...]), NN)), TN)
            t1 = split2(x1)
            x2 = v2[:, r:] - dot3(split2(v2[:, :r]), t1, NN)
            t2 = split2(x2)
            x3 = v3[:, 2 * r :] - dot3(split2(v3[:, :r]), t2, NN)
            x3 = x3 - dot3(split2(v3[:, r : 2 * r]), t1, NN)
            x[0:r, :] = x3
            x[r : 2 * r, :] = x2
            x[2 * r :, :] = x1
            core_block(core1, 2, 4)

    def one_level(level, carry):
        l3 = [l_parts[level, n] for n in range(3)]
        lt3 = [lt_parts[level, n] for n in range(3)]
        g3 = split3(g[level])
        gl = jnp.concatenate(
            [
                dot6([y[at] for y in g3], [y[at] for y in l3], NN)
                for at in (slice(0, r), slice(r, order))
            ],
            0,
        )
        gl3 = split3(gl)
        for o in range(0, order, NB):
            at = slice(o, o + NB)
            c[at, o:order] = dot6([y[at] for y in lt3], [y[:, o:] for y in gl3], NN)
            c[at, order:] = turned[level, at, :]
        work[...] = c[0:NB, 0:NB] + eye
        behind = None
        for j in range(steps):
            o = j * NB
            t = o + NB
            u = t + NB
            if behind is not None:
                behind()
            invert_factor(work, spread)
            inverse = split3(work[...])
            if t < order:
                near_row = split3(dot6(inverse, split3(c[o:t, t:u]), NN))
                work[...] = c[t:u, t:u] - dot6(near_row, near_row, TN) + eye

                def behind(o=o, t=t, u=u, inverse=inverse, near_row=near_row):
                    out = dot6(inverse, split3(c[o:t, u:]), NN)
                    m[o:t, :] = out[:, order - u :]
                    out3 = split3(out)
                    c[t:u, u:] = c[t:u, u:] - dot6(near_row, out3, TN)
                    for w in range(u, order, NB):
                        a = w - u
                        c[w : w + NB, w:] = c[w : w + NB, w:] - dot6(
                            [y[:, a : a + NB] for y in out3], [y[:, a:] for y in out3], TN
                        )

            else:
                m[o:t, :] = dot6(inverse, split3(c[o:t, order:]), NN)
            for lv, jj in ((0, 0), (0, 1), (0, 2), (0, 3), (1, 0), (1, 1), (1, 2), (2, 1)):
                if jj == j:

                    @pl.when(level == lv)
                    def _(lv=lv, jj=jj):
                        hook(lv, jj)

        for lv in range(3):

            @pl.when(level == lv)
            def _(lv=lv):
                after(lv)

        return carry

    lax.fori_loop(0, 3, one_level, 0)
    sends = [*nears, *g_gather, *g_shares, *across, ex_g[1], ex_g[2], sh_g[1], sh_g[2], sh_s]
    sends += [*sh_q[1], *sh_q[2], *wide_q1, *wide_q2, *s1_gather, tail_swap]
    for copies in (*scatters, *gathers, *bag_shares):
        sends += copies
    for copy in sends:
        copy.wait_send()


def mega(b3, b2, b1, rhs, leaf, cpl3, cpl2, cpl1):
    rows, r = b3.shape
    order = 2 * r
    chips = lax.axis_size("gy") // 2
    hr = r // 2
    pr = hr // chips
    most = max(len(y) for y in GROUPS)
    wide = pr + pr // 2
    hbm = pl.BlockSpec(memory_space=pl.ANY)
    dma = pltpu.SemaphoreType.DMA

    def vmem(*shape):
        return pltpu.VMEM(shape, F32)

    return pl.pallas_call(
        lambda *refs: mega_kernel(chips, *refs),
        in_specs=[hbm] * 4 + [VMEM] + [hbm] * 3,
        out_specs=[VMEM] * 4,
        out_shape=[
            jax.ShapeDtypeStruct(shape, F32)
            for shape in ((3 * r, r), (16, order), (8, order), (4, order))
        ],
        scratch_shapes=[
            vmem(4, rows, r),
            pltpu.VMEM((3, r, rows), BF16),
            pltpu.VMEM((3, r, rows), BF16),
            vmem(4, most, r, r),
            vmem(4, most, hr, r),
            vmem(4, most, hr, r),
            vmem(4, chips - 1, most, pr, r),
            vmem(4, most, pr, r),
            vmem(4, most - 1, pr, r),
            vmem(3, wide, r),
            vmem(3, 2, 2, chips, wide, r),
            vmem(3, order, r),
            vmem(order, 3 * r),
            vmem(2 * chips, 2, pr // 2, r),
            vmem(pr // 2, 4 * r),
            vmem(2, r, r),
            vmem(order, 2 * r),
            vmem(pr // 2, 2 * r),
            vmem(pr // 2, 2 * r),
            vmem(r, r),
            vmem(pr // 2, 2 * r),
            vmem(pr // 2, 2 * r),
            vmem(order, r),
            vmem(pr // 2, r),
            vmem(hr, 2 * r),
            vmem(3, order, order),
            vmem(3, order, order),
            pltpu.VMEM((3, 3, order, order), BF16),
            pltpu.VMEM((3, 3, order, order), BF16),
            vmem(order, 2 * order),
            vmem(NB, NB),
            vmem(W, W // 8, 8, NB),
            vmem(order, order),
            vmem(order, 3 * r),
            vmem(r, 3 * r),
            vmem(r, 2 * r),
            vmem(NB, order),
            dma((7,)),
            dma((2, 4)),
            dma((2, 4, chips - 1)),
            dma((2, 2 * chips - 1)),
            dma((2, 2)),
            dma((2, 4)),
            dma((2, 3, 2 * chips - 1)),
            dma((2, 3, 2)),
            dma((2, 3, 1)),
            dma((2, 3, 4)),
            dma((2, 4 * chips - 1)),
            dma((2, 2 * chips - 1)),
            dma((2,)),
            dma((2, 4 * chips - 1)),
        ],
        compiler_params=pltpu.CompilerParams(
            collective_id=0, has_side_effects=True, vmem_limit_bytes=60 << 20
        ),
        name="mega",
    )(b3, b2, b1, rhs, leaf.reshape(rows // 128, 128), cpl3, cpl2, cpl1)


def apply_kernel(b3, b2, b1, rhs, leaf, x, k3, k2, k1, out, core3, core2, core1):
    r = b3.shape[1]

    @pl.when(pl.program_id(0) == 0)
    def _():
        core3[...] = k3[...]
        core2[...] = k2[...]
        core1[...] = k1[...]

    xs = split2(x[...])
    total = rhs[...]
    for i, b in enumerate((b3, b2, b1)):
        total = total - dot3(split2(b[...]), tuple(y[i * r : (i + 1) * r] for y in xs), NN)
    turned = leaf[0].T
    out[...] = total * jnp.concatenate([turned[:, u : u + 1] for u in range(leaf.shape[1])], 0)


def apply_update(b3, b2, b1, rhs, leaf, x, cores):
    rows, r = b3.shape
    tile = 512
    block = pl.BlockSpec((tile, r), lambda i: (i, 0))
    whole = [pl.BlockSpec(k.shape, lambda i: (0, 0)) for k in cores]
    return pl.pallas_call(
        apply_kernel,
        grid=(rows // tile,),
        in_specs=[block] * 4
        + [
            pl.BlockSpec((1, tile // 128, 128), lambda i: (i, 0, 0)),
            pl.BlockSpec(x.shape, lambda i: (0, 0)),
        ]
        + whole,
        out_specs=[block] + whole,
        out_shape=[jax.ShapeDtypeStruct(rhs.shape, F32)]
        + [jax.ShapeDtypeStruct(k.shape, F32) for k in cores],
        name="apply_update",
    )(b3, b2, b1, rhs, leaf.reshape(rows // tile, tile // 128, 128), x, *cores)


def per_device(basis3, basis2, basis1, leaf_inverse, rhs, coupling3, coupling2, coupling1):
    x, *cores = mega(
        basis3, basis2, basis1, rhs, leaf_inverse, coupling3, coupling2, coupling1
    )
    return tuple(apply_update(basis3, basis2, basis1, rhs, leaf_inverse, x, cores))


def solution(mesh):
    rows = P(("gx", "gy"), None)
    return jax.shard_map(
        per_device,
        mesh=mesh,
        in_specs=(rows, rows, rows, P(("gx", "gy")), rows, P(), P(), P()),
        out_specs=(rows, rows, rows, rows),
        check_vma=False,
    )
```

```python
import jax
import jax.numpy as jnp
from jax import lax
from jax.experimental import pallas as pl
from jax.experimental.pallas import tpu as pltpu
from jax.sharding import PartitionSpec as P

F32 = jnp.float32
BF16 = jnp.bfloat16
NN = ((1,), (0,))
TN = ((0,), (0,))
W = 32
NB = 128
VMEM = pl.BlockSpec(memory_space=pltpu.VMEM)


def dot6(a, b, dims):
    (i,), (j,) = dims
    left = jnp.concatenate([a[0], a[0], a[1], a[0], a[2], a[1]], i)
    right = jnp.concatenate([b[0], b[1], b[0], b[2], b[0], b[1]], j)
    return dot1(left, right, dims)


def dot1(a, b, dims):
    return lax.dot_general(a, b, (dims, ((), ())), preferred_element_type=F32)


def split2(x):
    hi = x.astype(BF16)
    return hi, (x - hi.astype(F32)).astype(BF16)


def split3(x):
    hi = x.astype(BF16)
    rest = x - hi.astype(F32)
    mid = rest.astype(BF16)
    return hi, mid, (rest - mid.astype(F32)).astype(BF16)


def dot3(a, b, dims):
    (i,), (j,) = dims
    left = jnp.concatenate([a[0], a[0], a[1]], i)
    right = jnp.concatenate([b[0], b[1], b[0]], j)
    return dot1(left, right, dims)


MESH = pl.DeviceIdType.MESH


def where_am_i():
    gx = lax.axis_index("gx")
    gy = lax.axis_index("gy")
    core = gy % 2
    return gx, gy, core, gy // 2, gy + 1 - 2 * core, gx + 1 - 2 * (gx % 2)


def greet(peers):
    barrier = pltpu.get_barrier_semaphore()
    for peer in peers:
        pl.semaphore_signal(barrier, inc=1, device_id=peer, device_id_type=MESH)


def all_met(peers):
    pl.semaphore_wait(pltpu.get_barrier_semaphore(), len(peers))


def group_peers(chips):
    gx, gy, core, chip, other, sib = where_am_i()
    own = [(gx, 2 * ((chip + d) % chips) + core) for d in range(1, chips)]
    far = [(sib, 2 * ((chip + d) % chips) + core) for d in range(chips)]
    return [(gx, other)] + own + far


def remote(src, dst, send, recv, peer):
    return pltpu.make_async_remote_copy(
        src_ref=src, dst_ref=dst, send_sem=send, recv_sem=recv, device_id=peer, device_id_type=MESH
    )


def invert_factor(work, spread):
    n = work.shape[0]
    parts = W // 8
    lane = lax.broadcasted_iota(jnp.int32, (8, n), 1)
    sub = lax.broadcasted_iota(jnp.int32, (8, n), 0)
    wide = lax.broadcasted_iota(jnp.int32, (W, n), 1)
    for s in range(n // W):
        o = s * W
        block = [work[o + 8 * h : o + 8 * h + 8, :] for h in range(parts)]
        for k in range(W):
            for h in range(k // 8, parts):
                spread[k, h] = jnp.broadcast_to(block[h][:, o + k : o + k + 1], (8, n))
        col = {(k, h): spread[k, h] for k in range(W) for h in range(k // 8, parts)}
        inside = (lane >= o) & (lane < o + W)
        x = [
            jnp.where(inside, jnp.where(lane - o == sub + 8 * h, 1.0, 0.0), block[h])
            for h in range(parts)
        ]
        for k in range(W):
            g, e = k // 8, k % 8
            d = col[k, g][e : e + 1]
            recip = 1.0 / d
            pivot_row = x[g][e : e + 1]
            for h in range(g, parts):
                m = col[k, h] * recip
                if h == g:
                    m = jnp.where(sub > e, m, 0.0)
                for j in range(k + 1, min(W, 8 * h + 8)):
                    col[j, h] = col[j, h] - m * col[k, j // 8][j % 8 : j % 8 + 1]
                x[h] = x[h] - m * pivot_row
            x[g] = jnp.where(sub == e, x[g] * lax.rsqrt(d), x[g])
        v = jnp.concatenate(x, 0)
        work[o : o + W, :] = jnp.where(wide < o + W, v, 0.0)
        t = o + W
        if t < n:
            v3 = split3(v)
            update = dot6(v3, v3, TN)
            below = lax.broadcasted_iota(jnp.int32, (n - t, n), 1)
            kept = jnp.where((below >= o) & (below < t), 0.0, work[t:, :])
            work[t:, :] = kept - update[t:, :]


GROUPS = (((0, 0),), ((0, 1), (1, 1)), ((0, 2), (1, 2), (2, 2)), ((0, 3), (1, 3), (2, 3)))
ORDER = {(1, 0): 0, (2, 0): 1, (2, 1): 3, (3, 0): 2, (3, 1): 4}
TILE = 512


def mega_kernel(
    chips, b3, b2, b1, rhs, leaf, cpl3, cpl2, cpl1, x, core3, core2, core1,
    raw, hi_t, lo_t, part, near, half, arrived, piece, far, pay, bag, g, q, s, h, q1, s1, tail, q2,
    coupling, turned, l_parts, lt_parts, c, work, spread, m, p, v3, v2, krows,
    load_sem, near_sem, rs_sem, ag_sem, share_sem, far_sem, bag_sem, bshare_sem, ex_sem, exs_sem,
):
    gx, gy, core, chip, other, sib = where_am_i()
    rows, r = b3.shape
    order = 2 * r
    tiles = rows // TILE
    per = TILE // leaf.shape[1]
    hr = r // 2
    pr = hr // chips
    sides = (gx % 2, (gx // 2) % 2, (gx // 4) % 2)
    far_gx = (sib, gx + 2 - 4 * sides[1], gx + 4 - 8 * sides[2])
    side = sides[0]
    partner = (gx, other)

    loads = [
        pltpu.make_async_copy(b, raw.at[i], load_sem.at[i]) for i, b in enumerate((b3, b2, b1, rhs))
    ]
    loads += [
        pltpu.make_async_copy(src.at[at], coupling.at[i], load_sem.at[4 + i])
        for i, (src, at) in enumerate(((cpl3, gx // 2), (cpl2, gx // 4), (cpl1, 0)))
    ]
    loads[0].start()
    peers = group_peers(chips)
    everyone = peers + [(far_gx[1], gy), (far_gx[2], gy)]
    greet(everyone)
    for copy in loads[1:]:
        copy.start()
    root = jnp.sqrt(leaf[...]).T

    nears = [
        remote(
            part.at[i, pl.ds(0, len(GROUPS[i])), pl.ds(pl.multiple_of((1 - core) * hr, hr), hr), :],
            near.at[i, pl.ds(0, len(GROUPS[i]))],
            near_sem.at[0, i], near_sem.at[1, i], partner,
        )
        for i in range(4)
    ]
    scatters = [
        [
            remote(
                half.at[
                    i, pl.ds(0, len(GROUPS[i])),
                    pl.ds(pl.multiple_of(((chip + d) % chips) * pr, pr), pr), :,
                ],
                arrived.at[i, d - 1, pl.ds(0, len(GROUPS[i]))],
                rs_sem.at[0, i, d - 1], rs_sem.at[1, i, d - 1], peers[d],
            )
            for d in range(1, chips)
        ]
        for i in range(4)
    ]
    row = pl.multiple_of(side * r + core * hr + chip * pr, pr)
    g_gather = [
        remote(
            piece.at[0, 0], g.at[0, pl.ds(row, pr), :], ag_sem.at[0, d], ag_sem.at[1, d], peer
        )
        for d, peer in enumerate(peers[1:])
    ]
    g_shares = []
    for t in range(2):
        at = g.at[0, pl.ds(pl.multiple_of(t * r + core * hr, hr), hr), :]
        g_shares.append(remote(at, at, share_sem.at[0, t], share_sem.at[1, t], partner))
    across = [
        remote(
            piece.at[i, pl.ds(0, len(GROUPS[i]))], far.at[i, pl.ds(0, len(GROUPS[i]))],
            far_sem.at[0, i], far_sem.at[1, i], (sib, gy),
        )
        for i in range(1, 4)
    ]
    bag_rows = [pr * (len(GROUPS[i]) + 1) for i in range(1, 4)]
    gathers = [
        [
            remote(
                pay.at[i, pl.ds(0, n), :], bag.at[i, core, chip, pl.ds(0, n), :],
                bag_sem.at[0, i, d], bag_sem.at[1, i, d], peer,
            )
            for d, peer in enumerate(peers[1:chips])
        ]
        for i, n in enumerate(bag_rows)
    ]
    bag_shares = [
        remote(
            bag.at[i, core, :, pl.ds(0, n), :], bag.at[i, core, :, pl.ds(0, n), :],
            bshare_sem.at[0, i], bshare_sem.at[1, i], partner,
        )
        for i, n in enumerate(bag_rows)
    ]

    def local(i):
        loads[i].wait()
        n = len(GROUPS[i])
        for t in range(tiles):
            at = slice(t * TILE, (t + 1) * TILE)
            scale = jnp.concatenate([root[:, t * per + u : t * per + u + 1] for u in range(per)], 0)
            upper, lower = split2(raw[i, at, :] * scale)
            if i < 3:
                hi_t[i, :, at] = upper.T
                lo_t[i, :, at] = lower.T
            left = tuple(
                jnp.concatenate([z[a, :, at] for a, b in GROUPS[i]], 0) for z in (hi_t, lo_t)
            )
            sums = dot3(left, (upper, lower), NN).reshape(n, r, r)
            part[i, 0:n] = sums if t == 0 else part[i, 0:n] + sums
        if i == 0:
            all_met(everyone)
        nears[i].start()

    def scatter(i):
        n = len(GROUPS[i])
        nears[i].wait_recv()
        half[i, 0:n] = part[i, 0:n, pl.ds(pl.multiple_of(core * hr, hr), hr), :] + near[i, 0:n]
        for copy in scatters[i]:
            copy.start()

    def collect(i):
        n = len(GROUPS[i])
        total = half[i, 0:n, pl.ds(pl.multiple_of(chip * pr, pr), pr), :]
        for d, copy in enumerate(scatters[i]):
            copy.wait_recv()
            total = total + arrived[i, d, 0:n]
        piece[i, 0:n] = total
        if i > 0:
            across[i - 1].start()

    def gather(i):
        across[i - 1].wait_recv()
        own_at = pl.ds(pl.multiple_of(side * pr, pr), pr)
        far_at = pl.ds(pl.multiple_of((1 - side) * pr, pr), pr)
        pay[i - 1, own_at, :] = piece[i, 0]
        pay[i - 1, far_at, :] = far[i, 0]
        for n in range(1, len(GROUPS[i])):
            pay[i - 1, (n + 1) * pr : (n + 2) * pr, :] = piece[i, n] + far[i, n]
        for copy in gathers[i - 1]:
            copy.start()
        bag[i - 1, core, chip, 0 : bag_rows[i - 1], :] = pay[i - 1, 0 : bag_rows[i - 1], :]

    def share(i):
        for copy in gathers[i - 1]:
            copy.wait_recv()
        bag_shares[i - 1].start()

    def unpack(i):
        bag_shares[i - 1].wait_recv()
        for t in range(2):
            q[t * r : (t + 1) * r, (i - 1) * r : i * r] = bag[
                i - 1, :, :, t * pr : (t + 1) * pr, :
            ].reshape(r, r)
        for n in range(1, len(GROUPS[i])):
            s[ORDER[i, n - 1]] = bag[i - 1, :, :, (n + 1) * pr : (n + 2) * pr, :].reshape(r, r)

    def swap(level, src, dst, n):
        return remote(src, dst, ex_sem.at[0, level, n], ex_sem.at[1, level, n], (far_gx[level], gy))

    def pass_on(level, ref, n):
        return remote(ref, ref, exs_sem.at[0, level, n], exs_sem.at[1, level, n], partner)

    mine = pl.ds(pl.multiple_of(core * hr, hr), hr)
    ex_g, ex_q, sh_g, sh_q = {}, {}, {}, {}
    ch = hr // 2
    for level, qs in ((1, q1), (2, q2)):
        base = sides[level] * r + core * hr
        away = (1 - sides[level]) * r + core * hr
        to = pl.ds(pl.multiple_of(base, hr), hr)
        come = pl.ds(pl.multiple_of(away, hr), hr)
        ex_g[level], sh_g[level] = [], []
        for n in range(2):
            from_at = pl.ds(pl.multiple_of(core * hr + n * ch, ch), ch)
            to_at = pl.ds(pl.multiple_of(base + n * ch, ch), ch)
            come_at = pl.ds(pl.multiple_of(away + n * ch, ch), ch)
            ex_g[level].append(swap(level, h.at[level - 1, 0, from_at, :], g.at[level, to_at, :], 3 * n))
            sh_g[level].append(pass_on(level, g.at[level, come_at, :], 3 * n))
        ex_q[level] = swap(level, qs.at[to, :], qs.at[to, :], 1)
        sh_q[level] = pass_on(level, qs.at[come, :], 1)
    ex_s = swap(1, s1.at[mine, :], tail, 2)
    sh_s = pass_on(1, s1.at[mine, :], 2)

    def prepare(level):
        loads[4 + level].wait()
        across_rows = coupling[level].T
        turned[level] = across_rows
        for n, (y, z) in enumerate(zip(split3(coupling[level]), split3(across_rows))):
            l_parts[level, n] = y
            lt_parts[level, n] = z

    local(0)
    local(1)
    scatter(0)
    local(2)
    collect(0)
    g[0, pl.ds(row, pr), :] = piece[0, 0]
    for copy in g_gather:
        copy.start()
    scatter(1)
    local(3)
    scatter(2)
    collect(1)
    for copy in g_gather:
        copy.wait_recv()
    for copy in g_shares:
        copy.start()
    scatter(3)
    gather(1)
    collect(2)
    prepare(0)
    for copy in g_shares:
        copy.wait_recv()

    eye = jnp.where(
        lax.broadcasted_iota(jnp.int32, (NB, NB), 0) == lax.broadcasted_iota(jnp.int32, (NB, NB), 1),
        1.0,
        0.0,
    )
    steps = order // NB

    def receive_q(level):
        ex_q[level].wait_recv()
        sh_q[level].start()

    def hook(level, j):
        if (level, j) == (0, 0):
            gather(2)
            collect(3)
        elif (level, j) == (0, 1):
            gather(3)
            share(1)
        elif (level, j) == (0, 2):
            share(2)
        elif (level, j) == (0, 3):
            share(3)
            unpack(1)
        elif (level, j) == (1, 2):
            receive_q(1)
        elif (level, j) == (1, 3):
            ex_s.wait()
            s1[mine, :] = s1[mine, :] + tail[...]
            sh_s.start()
        elif (level, j) == (2, 1):
            receive_q(2)

    def core_block(out, level, count):
        place = gx * 2 * chips + gy
        start = (place % (4 * chips << level)) * count
        at = pl.ds(pl.multiple_of((start // NB) * NB, NB), NB)
        krows[...] = dot3(split2(m[:, at]), split2(m[...]), TN)
        inner = start % NB
        if count % 8 == 0:
            out[...] = krows[pl.ds(pl.multiple_of(inner, 8), count), :]
        else:
            eight = krows[pl.ds(pl.multiple_of((inner // 8) * 8, 8), 8), :]
            out[...] = jnp.where(inner % 8 == 0, eight[:count], eight[count:])

    def own_of(level):
        return split2(m[:, pl.ds(pl.multiple_of(sides[level] * r, r), r)])

    def column(i):
        return split2(p[:, i * r : (i + 1) * r])

    def after(level):
        ms = split2(m[...])
        if level == 0:
            p[:, 0:r] = dot3(ms, split2(q[:, 0:r]), NN)
            p2 = column(0)
            h[0, 0] = s[0] - dot3(p2, p2, TN)
            for copy in ex_g[1]:
                copy.start()
            g[1, pl.ds(pl.multiple_of(sides[1] * r, r), r), :] = h[0, 0]
            unpack(2)
            unpack(3)
            p[:, r:] = dot3(ms, split2(q[:, r:]), NN)
            p1, pc = column(1), column(2)
            at = pl.ds(pl.multiple_of(sides[1] * r, r), r)
            q1[at, 0:r] = s[1] - dot3(p2, p1, TN)
            q1[at, r:] = s[2] - dot3(p2, pc, TN)
            ex_q[1].start()
            s1[:, 0:r] = s[3] - dot3(p1, p1, TN)
            s1[:, r:] = s[4] - dot3(p1, pc, TN)
            ex_s.start()
            prepare(1)
            for come_in, hand_on in zip(ex_g[1], sh_g[1]):
                come_in.wait_recv()
                hand_on.start()
            v3[...] = dot3(own_of(0), split2(p[...]), TN)
            core_block(core3, 0, 16)
            for copy in sh_g[1]:
                copy.wait_recv()
        elif level == 1:
            sh_q[1].wait_recv()
            p[:, 0:r] = dot3(ms, split2(q1[:, 0:r]), NN)
            p1 = column(0)
            sh_s.wait_recv()
            h[1, 0] = s1[:, 0:r] - dot3(p1, p1, TN)
            for copy in ex_g[2]:
                copy.start()
            g[2, pl.ds(pl.multiple_of(sides[2] * r, r), r), :] = h[1, 0]
            p[:, r : 2 * r] = dot3(ms, split2(q1[:, r:]), NN)
            q2[pl.ds(pl.multiple_of(sides[2] * r, r), r), :] = s1[:, r:] - dot3(p1, column(1), TN)
            ex_q[2].start()
            prepare(2)
            for come_in, hand_on in zip(ex_g[2], sh_g[2]):
                come_in.wait_recv()
                hand_on.start()
            v2[...] = dot3(own_of(1), split2(p[:, 0 : 2 * r]), TN)
            core_block(core2, 1, 8)
            for copy in sh_g[2]:
                copy.wait_recv()
        else:
            sh_q[2].wait_recv()
            x1 = dot3(own_of(2), split2(dot3(ms, split2(q2[...]), NN)), TN)
            t1 = split2(x1)
            x2 = v2[:, r:] - dot3(split2(v2[:, :r]), t1, NN)
            t2 = split2(x2)
            x3 = v3[:, 2 * r :] - dot3(split2(v3[:, :r]), t2, NN)
            x3 = x3 - dot3(split2(v3[:, r : 2 * r]), t1, NN)
            x[0:r, :] = x3
            x[r : 2 * r, :] = x2
            x[2 * r :, :] = x1
            core_block(core1, 2, 4)

    def one_level(level, carry):
        l3 = [l_parts[level, n] for n in range(3)]
        lt3 = [lt_parts[level, n] for n in range(3)]
        g3 = split3(g[level])
        gl = jnp.concatenate(
            [
                dot6([y[at] for y in g3], [y[at] for y in l3], NN)
                for at in (slice(0, r), slice(r, order))
            ],
            0,
        )
        gl3 = split3(gl)
        for o in range(0, order, NB):
            at = slice(o, o + NB)
            c[at, o:order] = dot6([y[at] for y in lt3], [y[:, o:] for y in gl3], NN)
            c[at, order:] = turned[level, at, :]
        work[...] = c[0:NB, 0:NB] + eye
        behind = None
        for j in range(steps):
            o = j * NB
            t = o + NB
            u = t + NB
            if behind is not None:
                behind()
            invert_factor(work, spread)
            inverse = split3(work[...])
            if t < order:
                near_row = split3(dot6(inverse, split3(c[o:t, t:u]), NN))
                work[...] = c[t:u, t:u] - dot6(near_row, near_row, TN) + eye

                def behind(o=o, t=t, u=u, inverse=inverse, near_row=near_row):
                    out = dot6(inverse, split3(c[o:t, u:]), NN)
                    m[o:t, :] = out[:, order - u :]
                    out3 = split3(out)
                    c[t:u, u:] = c[t:u, u:] - dot6(near_row, out3, TN)
                    for w in range(u, order, NB):
                        a = w - u
                        c[w : w + NB, w:] = c[w : w + NB, w:] - dot6(
                            [y[:, a : a + NB] for y in out3], [y[:, a:] for y in out3], TN
                        )

            else:
                m[o:t, :] = dot6(inverse, split3(c[o:t, order:]), NN)
            for lv, jj in ((0, 0), (0, 1), (0, 2), (0, 3), (1, 2), (1, 3), (2, 1)):
                if jj == j:

                    @pl.when(level == lv)
                    def _(lv=lv, jj=jj):
                        hook(lv, jj)

        for lv in range(3):

            @pl.when(level == lv)
            def _(lv=lv):
                after(lv)

        return carry

    lax.fori_loop(0, 3, one_level, 0)
    sends = [*nears, *g_gather, *g_shares, *across, *ex_g[1], *ex_g[2], ex_q[1], ex_q[2]]
    sends += [*sh_g[1], *sh_g[2], sh_q[1], sh_q[2], sh_s, *bag_shares]
    for copies in (*scatters, *gathers):
        sends += copies
    for copy in sends:
        copy.wait_send()


def mega(b3, b2, b1, rhs, leaf, cpl3, cpl2, cpl1):
    rows, r = b3.shape
    order = 2 * r
    chips = lax.axis_size("gy") // 2
    hr = r // 2
    pr = hr // chips
    most = max(len(y) for y in GROUPS)
    wide = pr * (most + 1)
    hbm = pl.BlockSpec(memory_space=pl.ANY)
    dma = pltpu.SemaphoreType.DMA

    def vmem(*shape):
        return pltpu.VMEM(shape, F32)

    return pl.pallas_call(
        lambda *refs: mega_kernel(chips, *refs),
        in_specs=[hbm] * 4 + [VMEM] + [hbm] * 3,
        out_specs=[VMEM] * 4,
        out_shape=[
            jax.ShapeDtypeStruct(shape, F32)
            for shape in ((3 * r, r), (16, order), (8, order), (4, order))
        ],
        scratch_shapes=[
            vmem(4, rows, r),
            pltpu.VMEM((3, r, rows), BF16),
            pltpu.VMEM((3, r, rows), BF16),
            vmem(4, most, r, r),
            vmem(4, most, hr, r),
            vmem(4, most, hr, r),
            vmem(4, chips - 1, most, pr, r),
            vmem(4, most, pr, r),
            vmem(4, most, pr, r),
            vmem(3, wide, r),
            vmem(3, 2, chips, wide, r),
            vmem(3, order, r),
            vmem(order, 3 * r),
            vmem(5, r, r),
            vmem(2, 1, r, r),
            vmem(order, 2 * r),
            vmem(r, 2 * r),
            vmem(hr, 2 * r),
            vmem(order, r),
            vmem(3, order, order),
            vmem(3, order, order),
            pltpu.VMEM((3, 3, order, order), BF16),
            pltpu.VMEM((3, 3, order, order), BF16),
            vmem(order, 2 * order),
            vmem(NB, NB),
            vmem(W, W // 8, 8, NB),
            vmem(order, order),
            vmem(order, 3 * r),
            vmem(r, 3 * r),
            vmem(r, 2 * r),
            vmem(NB, order),
            dma((7,)),
            dma((2, 4)),
            dma((2, 4, chips - 1)),
            dma((2, 2 * chips - 1)),
            dma((2, 2)),
            dma((2, 4)),
            dma((2, 3, chips - 1)),
            dma((2, 3)),
            dma((2, 3, 4)),
            dma((2, 3, 4)),
        ],
        compiler_params=pltpu.CompilerParams(
            collective_id=0, has_side_effects=True, vmem_limit_bytes=60 << 20
        ),
        name="mega",
    )(b3, b2, b1, rhs, leaf.reshape(rows // 128, 128), cpl3, cpl2, cpl1)


def apply_kernel(b3, b2, b1, rhs, leaf, x, k3, k2, k1, out, core3, core2, core1):
    r = b3.shape[1]

    @pl.when(pl.program_id(0) == 0)
    def _():
        core3[...] = k3[...]
        core2[...] = k2[...]
        core1[...] = k1[...]

    xs = split2(x[...])
    total = rhs[...]
    for i, b in enumerate((b3, b2, b1)):
        total = total - dot3(split2(b[...]), tuple(y[i * r : (i + 1) * r] for y in xs), NN)
    turned = leaf[0].T
    out[...] = total * jnp.concatenate([turned[:, u : u + 1] for u in range(leaf.shape[1])], 0)


def apply_update(b3, b2, b1, rhs, leaf, x, cores):
    rows, r = b3.shape
    tile = 512
    block = pl.BlockSpec((tile, r), lambda i: (i, 0))
    whole = [pl.BlockSpec(k.shape, lambda i: (0, 0)) for k in cores]
    return pl.pallas_call(
        apply_kernel,
        grid=(rows // tile,),
        in_specs=[block] * 4
        + [
            pl.BlockSpec((1, tile // 128, 128), lambda i: (i, 0, 0)),
            pl.BlockSpec(x.shape, lambda i: (0, 0)),
        ]
        + whole,
        out_specs=[block] + whole,
        out_shape=[jax.ShapeDtypeStruct(rhs.shape, F32)]
        + [jax.ShapeDtypeStruct(k.shape, F32) for k in cores],
        name="apply_update",
    )(b3, b2, b1, rhs, leaf.reshape(rows // tile, tile // 128, 128), x, *cores)


def per_device(basis3, basis2, basis1, leaf_inverse, rhs, coupling3, coupling2, coupling1):
    x, *cores = mega(
        basis3, basis2, basis1, rhs, leaf_inverse, coupling3, coupling2, coupling1
    )
    return tuple(apply_update(basis3, basis2, basis1, rhs, leaf_inverse, x, cores))


def solution(mesh):
    rows = P(("gx", "gy"), None)
    return jax.shard_map(
        per_device,
        mesh=mesh,
        in_specs=(rows, rows, rows, P(("gx", "gy")), rows, P(), P(), P()),
        out_specs=(rows, rows, rows, rows),
        check_vma=False,
    )
```

```python
import jax
import jax.numpy as jnp
from jax import lax
from jax.experimental import pallas as pl
from jax.experimental.pallas import tpu as pltpu
from jax.sharding import PartitionSpec as P

F32 = jnp.float32
BF16 = jnp.bfloat16
NN = ((1,), (0,))
TN = ((0,), (0,))
W = 32
NB = 128
VMEM = pl.BlockSpec(memory_space=pltpu.VMEM)


def dot6(a, b, dims):
    (i,), (j,) = dims
    left = jnp.concatenate([a[0], a[0], a[1], a[0], a[2], a[1]], i)
    right = jnp.concatenate([b[0], b[1], b[0], b[2], b[0], b[1]], j)
    return dot1(left, right, dims)


def dot1(a, b, dims):
    return lax.dot_general(a, b, (dims, ((), ())), preferred_element_type=F32)


def split2(x):
    hi = x.astype(BF16)
    return hi, (x - hi.astype(F32)).astype(BF16)


def split3(x):
    hi = x.astype(BF16)
    rest = x - hi.astype(F32)
    mid = rest.astype(BF16)
    return hi, mid, (rest - mid.astype(F32)).astype(BF16)


def dot3(a, b, dims):
    (i,), (j,) = dims
    left = jnp.concatenate([a[0], a[0], a[1]], i)
    right = jnp.concatenate([b[0], b[1], b[0]], j)
    return dot1(left, right, dims)


MESH = pl.DeviceIdType.MESH


def where_am_i():
    gx = lax.axis_index("gx")
    gy = lax.axis_index("gy")
    core = gy % 2
    return gx, gy, core, gy // 2, gy + 1 - 2 * core, gx + 1 - 2 * (gx % 2)


def greet(peers):
    barrier = pltpu.get_barrier_semaphore()
    for peer in peers:
        pl.semaphore_signal(barrier, inc=1, device_id=peer, device_id_type=MESH)


def all_met(peers):
    pl.semaphore_wait(pltpu.get_barrier_semaphore(), len(peers))


def group_peers(chips):
    gx, gy, core, chip, other, sib = where_am_i()
    own = [(gx, 2 * ((chip + d) % chips) + core) for d in range(1, chips)]
    far = [(sib, 2 * ((chip + d) % chips) + core) for d in range(chips)]
    return [(gx, other)] + own + far


def remote(src, dst, send, recv, peer):
    return pltpu.make_async_remote_copy(
        src_ref=src, dst_ref=dst, send_sem=send, recv_sem=recv, device_id=peer, device_id_type=MESH
    )


def invert_factor(work, spread):
    n = work.shape[0]
    parts = W // 8
    lane = lax.broadcasted_iota(jnp.int32, (8, n), 1)
    sub = lax.broadcasted_iota(jnp.int32, (8, n), 0)
    wide = lax.broadcasted_iota(jnp.int32, (W, n), 1)
    for s in range(n // W):
        o = s * W
        block = [work[o + 8 * h : o + 8 * h + 8, :] for h in range(parts)]
        for k in range(W):
            for h in range(k // 8, parts):
                spread[k, h] = jnp.broadcast_to(block[h][:, o + k : o + k + 1], (8, n))
        col = {(k, h): spread[k, h] for k in range(W) for h in range(k // 8, parts)}
        inside = (lane >= o) & (lane < o + W)
        x = [
            jnp.where(inside, jnp.where(lane - o == sub + 8 * h, 1.0, 0.0), block[h])
            for h in range(parts)
        ]
        for k in range(W):
            g, e = k // 8, k % 8
            d = col[k, g][e : e + 1]
            recip = 1.0 / d
            pivot_row = x[g][e : e + 1]
            for h in range(g, parts):
                m = col[k, h] * recip
                if h == g:
                    m = jnp.where(sub > e, m, 0.0)
                for j in range(k + 1, min(W, 8 * h + 8)):
                    col[j, h] = col[j, h] - m * col[k, j // 8][j % 8 : j % 8 + 1]
                x[h] = x[h] - m * pivot_row
            x[g] = jnp.where(sub == e, x[g] * lax.rsqrt(d), x[g])
        v = jnp.concatenate(x, 0)
        work[o : o + W, :] = jnp.where(wide < o + W, v, 0.0)
        t = o + W
        if t < n:
            v3 = split3(v)
            update = dot6(v3, v3, TN)
            below = lax.broadcasted_iota(jnp.int32, (n - t, n), 1)
            kept = jnp.where((below >= o) & (below < t), 0.0, work[t:, :])
            work[t:, :] = kept - update[t:, :]


GROUPS = (((0, 0),), ((0, 1), (1, 1)), ((0, 2), (1, 2), (2, 2)), ((0, 3), (1, 3), (2, 3)))
ORDER = {(1, 0): 0, (2, 0): 1, (2, 1): 3, (3, 0): 2, (3, 1): 4}
TILE = 512


def mega_kernel(
    chips, b3, b2, b1, rhs, leaf, cpl3, cpl2, cpl1, x, core3, core2, core1,
    raw, hi_t, lo_t, part, near, half, arrived, piece, far, pay, bag, g, q, s, h, q1, s1, tail, q2,
    coupling, turned, l_parts, lt_parts, c, work, spread, m, p, v3, v2, krows,
    load_sem, near_sem, rs_sem, ag_sem, share_sem, far_sem, bag_sem, bshare_sem, ex_sem, exs_sem,
):
    gx, gy, core, chip, other, sib = where_am_i()
    rows, r = b3.shape
    order = 2 * r
    tiles = rows // TILE
    per = TILE // leaf.shape[1]
    hr = r // 2
    pr = hr // chips
    sides = (gx % 2, (gx // 2) % 2, (gx // 4) % 2)
    far_gx = (sib, gx + 2 - 4 * sides[1], gx + 4 - 8 * sides[2])
    side = sides[0]
    partner = (gx, other)

    loads = [
        pltpu.make_async_copy(b, raw.at[i], load_sem.at[i]) for i, b in enumerate((b3, b2, b1, rhs))
    ]
    loads += [
        pltpu.make_async_copy(src.at[at], coupling.at[i], load_sem.at[4 + i])
        for i, (src, at) in enumerate(((cpl3, gx // 2), (cpl2, gx // 4), (cpl1, 0)))
    ]
    loads[0].start()
    peers = group_peers(chips)
    everyone = peers + [(far_gx[1], gy), (far_gx[2], gy)]
    greet(everyone)
    root = jnp.sqrt(leaf[...]).T

    nears = [
        remote(
            part.at[i, pl.ds(0, len(GROUPS[i])), pl.ds(pl.multiple_of((1 - core) * hr, hr), hr), :],
            near.at[i, pl.ds(0, len(GROUPS[i]))],
            near_sem.at[0, i], near_sem.at[1, i], partner,
        )
        for i in range(4)
    ]
    scatters = [
        [
            remote(
                half.at[
                    i, pl.ds(0, len(GROUPS[i])),
                    pl.ds(pl.multiple_of(((chip + d) % chips) * pr, pr), pr), :,
                ],
                arrived.at[i, d - 1, pl.ds(0, len(GROUPS[i]))],
                rs_sem.at[0, i, d - 1], rs_sem.at[1, i, d - 1], peers[d],
            )
            for d in range(1, chips)
        ]
        for i in range(4)
    ]
    row = pl.multiple_of(side * r + core * hr + chip * pr, pr)
    g_gather = [
        remote(
            piece.at[0, 0], g.at[0, pl.ds(row, pr), :], ag_sem.at[0, d], ag_sem.at[1, d], peer
        )
        for d, peer in enumerate(peers[1:])
    ]
    g_shares = []
    for t in range(2):
        at = g.at[0, pl.ds(pl.multiple_of(t * r + core * hr, hr), hr), :]
        g_shares.append(remote(at, at, share_sem.at[0, t], share_sem.at[1, t], partner))
    across = [
        remote(
            piece.at[i, pl.ds(0, len(GROUPS[i]))], far.at[i, pl.ds(0, len(GROUPS[i]))],
            far_sem.at[0, i], far_sem.at[1, i], (sib, gy),
        )
        for i in range(1, 4)
    ]
    bag_rows = [pr * (len(GROUPS[i]) + 1) for i in range(1, 4)]
    gathers = [
        [
            remote(
                pay.at[i, pl.ds(0, n), :], bag.at[i, core, chip, pl.ds(0, n), :],
                bag_sem.at[0, i, d], bag_sem.at[1, i, d], peer,
            )
            for d, peer in enumerate(peers[1:chips])
        ]
        for i, n in enumerate(bag_rows)
    ]
    bag_shares = [
        remote(
            bag.at[i, core, :, pl.ds(0, n), :], bag.at[i, core, :, pl.ds(0, n), :],
            bshare_sem.at[0, i], bshare_sem.at[1, i], partner,
        )
        for i, n in enumerate(bag_rows)
    ]

    def local(i):
        loads[i].wait()
        for copy in (loads[1:4], loads[4:], [], [])[i]:
            copy.start()
        n = len(GROUPS[i])
        for t in range(tiles):
            at = slice(t * TILE, (t + 1) * TILE)
            scale = jnp.concatenate([root[:, t * per + u : t * per + u + 1] for u in range(per)], 0)
            upper, lower = split2(raw[i, at, :] * scale)
            if i < 3:
                hi_t[i, :, at] = upper.T
                lo_t[i, :, at] = lower.T
            left = tuple(
                jnp.concatenate([z[a, :, at] for a, b in GROUPS[i]], 0) for z in (hi_t, lo_t)
            )
            sums = dot3(left, (upper, lower), NN).reshape(n, r, r)
            part[i, 0:n] = sums if t == 0 else part[i, 0:n] + sums
        if i == 0:
            all_met(everyone)
        nears[i].start()

    def scatter(i):
        n = len(GROUPS[i])
        nears[i].wait_recv()
        half[i, 0:n] = part[i, 0:n, pl.ds(pl.multiple_of(core * hr, hr), hr), :] + near[i, 0:n]
        for copy in scatters[i]:
            copy.start()

    def collect(i):
        n = len(GROUPS[i])
        total = half[i, 0:n, pl.ds(pl.multiple_of(chip * pr, pr), pr), :]
        for d, copy in enumerate(scatters[i]):
            copy.wait_recv()
            total = total + arrived[i, d, 0:n]
        piece[i, 0:n] = total
        if i > 0:
            across[i - 1].start()

    def gather(i):
        across[i - 1].wait_recv()
        own_at = pl.ds(pl.multiple_of(side * pr, pr), pr)
        far_at = pl.ds(pl.multiple_of((1 - side) * pr, pr), pr)
        pay[i - 1, own_at, :] = piece[i, 0]
        pay[i - 1, far_at, :] = far[i, 0]
        for n in range(1, len(GROUPS[i])):
            pay[i - 1, (n + 1) * pr : (n + 2) * pr, :] = piece[i, n] + far[i, n]
        for copy in gathers[i - 1]:
            copy.start()
        bag[i - 1, core, chip, 0 : bag_rows[i - 1], :] = pay[i - 1, 0 : bag_rows[i - 1], :]

    def share(i):
        for copy in gathers[i - 1]:
            copy.wait_recv()
        bag_shares[i - 1].start()

    def unpack(i):
        bag_shares[i - 1].wait_recv()
        for t in range(2):
            q[t * r : (t + 1) * r, (i - 1) * r : i * r] = bag[
                i - 1, :, :, t * pr : (t + 1) * pr, :
            ].reshape(r, r)
        for n in range(1, len(GROUPS[i])):
            s[ORDER[i, n - 1]] = bag[i - 1, :, :, (n + 1) * pr : (n + 2) * pr, :].reshape(r, r)

    def swap(level, src, dst, n):
        return remote(src, dst, ex_sem.at[0, level, n], ex_sem.at[1, level, n], (far_gx[level], gy))

    def pass_on(level, ref, n):
        return remote(ref, ref, exs_sem.at[0, level, n], exs_sem.at[1, level, n], partner)

    mine = pl.ds(pl.multiple_of(core * hr, hr), hr)
    ex_g, ex_q, sh_g, sh_q = {}, {}, {}, {}
    ch = hr // 2
    for level, qs in ((1, q1), (2, q2)):
        base = sides[level] * r + core * hr
        away = (1 - sides[level]) * r + core * hr
        to = pl.ds(pl.multiple_of(base, hr), hr)
        come = pl.ds(pl.multiple_of(away, hr), hr)
        ex_g[level], sh_g[level] = [], []
        for n in range(2):
            from_at = pl.ds(pl.multiple_of(core * hr + n * ch, ch), ch)
            to_at = pl.ds(pl.multiple_of(base + n * ch, ch), ch)
            come_at = pl.ds(pl.multiple_of(away + n * ch, ch), ch)
            ex_g[level].append(swap(level, h.at[level - 1, 0, from_at, :], g.at[level, to_at, :], 3 * n))
            sh_g[level].append(pass_on(level, g.at[level, come_at, :], 3 * n))
        ex_q[level] = swap(level, qs.at[to, :], qs.at[to, :], 1)
        sh_q[level] = pass_on(level, qs.at[come, :], 1)
    ex_s = swap(1, s1.at[mine, :], tail, 2)
    sh_s = pass_on(1, s1.at[mine, :], 2)

    def prepare(level):
        loads[4 + level].wait()
        across_rows = coupling[level].T
        turned[level] = across_rows
        for n, (y, z) in enumerate(zip(split3(coupling[level]), split3(across_rows))):
            l_parts[level, n] = y
            lt_parts[level, n] = z

    local(0)
    local(1)
    scatter(0)
    local(2)
    collect(0)
    g[0, pl.ds(row, pr), :] = piece[0, 0]
    for copy in g_gather:
        copy.start()
    scatter(1)
    local(3)
    scatter(2)
    collect(1)
    for copy in g_gather:
        copy.wait_recv()
    for copy in g_shares:
        copy.start()
    scatter(3)
    gather(1)
    collect(2)
    prepare(0)
    for copy in g_shares:
        copy.wait_recv()

    eye = jnp.where(
        lax.broadcasted_iota(jnp.int32, (NB, NB), 0) == lax.broadcasted_iota(jnp.int32, (NB, NB), 1),
        1.0,
        0.0,
    )
    steps = order // NB

    def receive_q(level):
        ex_q[level].wait_recv()
        sh_q[level].start()

    def hook(level, j):
        if (level, j) == (0, 0):
            gather(2)
            collect(3)
        elif (level, j) == (0, 1):
            gather(3)
            share(1)
        elif (level, j) == (0, 2):
            share(2)
        elif (level, j) == (0, 3):
            share(3)
            unpack(1)
        elif (level, j) == (1, 2):
            receive_q(1)
        elif (level, j) == (1, 3):
            ex_s.wait()
            s1[mine, :] = s1[mine, :] + tail[...]
            sh_s.start()
        elif (level, j) == (2, 1):
            receive_q(2)

    def core_block(out, level, count):
        place = gx * 2 * chips + gy
        start = (place % (4 * chips << level)) * count
        at = pl.ds(pl.multiple_of((start // NB) * NB, NB), NB)
        krows[...] = dot3(split2(m[:, at]), split2(m[...]), TN)
        inner = start % NB
        if count % 8 == 0:
            out[...] = krows[pl.ds(pl.multiple_of(inner, 8), count), :]
        else:
            eight = krows[pl.ds(pl.multiple_of((inner // 8) * 8, 8), 8), :]
            out[...] = jnp.where(inner % 8 == 0, eight[:count], eight[count:])

    def own_of(level):
        return split2(m[:, pl.ds(pl.multiple_of(sides[level] * r, r), r)])

    def column(i):
        return split2(p[:, i * r : (i + 1) * r])

    def after(level):
        ms = split2(m[...])
        if level == 0:
            p[:, 0:r] = dot3(ms, split2(q[:, 0:r]), NN)
            p2 = column(0)
            h[0, 0] = s[0] - dot3(p2, p2, TN)
            for copy in ex_g[1]:
                copy.start()
            g[1, pl.ds(pl.multiple_of(sides[1] * r, r), r), :] = h[0, 0]
            unpack(2)
            unpack(3)
            p[:, r:] = dot3(ms, split2(q[:, r:]), NN)
            p1, pc = column(1), column(2)
            at = pl.ds(pl.multiple_of(sides[1] * r, r), r)
            q1[at, 0:r] = s[1] - dot3(p2, p1, TN)
            q1[at, r:] = s[2] - dot3(p2, pc, TN)
            ex_q[1].start()
            s1[:, 0:r] = s[3] - dot3(p1, p1, TN)
            s1[:, r:] = s[4] - dot3(p1, pc, TN)
            ex_s.start()
            prepare(1)
            v3[...] = dot3(own_of(0), split2(p[...]), TN)
            for come_in, hand_on in zip(ex_g[1], sh_g[1]):
                come_in.wait_recv()
                hand_on.start()
            core_block(core3, 0, 16)
            for copy in sh_g[1]:
                copy.wait_recv()
        elif level == 1:
            sh_q[1].wait_recv()
            p[:, 0:r] = dot3(ms, split2(q1[:, 0:r]), NN)
            p1 = column(0)
            sh_s.wait_recv()
            h[1, 0] = s1[:, 0:r] - dot3(p1, p1, TN)
            for copy in ex_g[2]:
                copy.start()
            g[2, pl.ds(pl.multiple_of(sides[2] * r, r), r), :] = h[1, 0]
            p[:, r : 2 * r] = dot3(ms, split2(q1[:, r:]), NN)
            q2[pl.ds(pl.multiple_of(sides[2] * r, r), r), :] = s1[:, r:] - dot3(p1, column(1), TN)
            ex_q[2].start()
            prepare(2)
            v2[...] = dot3(own_of(1), split2(p[:, 0 : 2 * r]), TN)
            for come_in, hand_on in zip(ex_g[2], sh_g[2]):
                come_in.wait_recv()
                hand_on.start()
            core_block(core2, 1, 8)
            for copy in sh_g[2]:
                copy.wait_recv()
        else:
            sh_q[2].wait_recv()
            x1 = dot3(own_of(2), split2(dot3(ms, split2(q2[...]), NN)), TN)
            t1 = split2(x1)
            x2 = v2[:, r:] - dot3(split2(v2[:, :r]), t1, NN)
            t2 = split2(x2)
            x3 = v3[:, 2 * r :] - dot3(split2(v3[:, :r]), t2, NN)
            x3 = x3 - dot3(split2(v3[:, r : 2 * r]), t1, NN)
            x[0:r, :] = x3
            x[r : 2 * r, :] = x2
            x[2 * r :, :] = x1
            core_block(core1, 2, 4)

    def one_level(level, carry):
        l3 = [l_parts[level, n] for n in range(3)]
        lt3 = [lt_parts[level, n] for n in range(3)]
        g3 = split3(g[level])
        gl = jnp.concatenate(
            [
                dot6([y[at] for y in g3], [y[at] for y in l3], NN)
                for at in (slice(0, r), slice(r, order))
            ],
            0,
        )
        gl3 = split3(gl)
        for o in range(0, order, NB):
            at = slice(o, o + NB)
            c[at, o:order] = dot6([y[at] for y in lt3], [y[:, o:] for y in gl3], NN)
            c[at, order:] = turned[level, at, :]
        work[...] = c[0:NB, 0:NB] + eye
        behind = None
        for j in range(steps):
            o = j * NB
            t = o + NB
            u = t + NB
            if behind is not None:
                behind()
            invert_factor(work, spread)
            inverse = split3(work[...])
            if t < order:
                near_row = split3(dot6(inverse, split3(c[o:t, t:u]), NN))
                work[...] = c[t:u, t:u] - dot6(near_row, near_row, TN) + eye

                def behind(o=o, t=t, u=u, inverse=inverse, near_row=near_row):
                    out = dot6(inverse, split3(c[o:t, u:]), NN)
                    m[o:t, :] = out[:, order - u :]
                    out3 = split3(out)
                    c[t:u, u:] = c[t:u, u:] - dot6(near_row, out3, TN)
                    for w in range(u, order, NB):
                        a = w - u
                        c[w : w + NB, w:] = c[w : w + NB, w:] - dot6(
                            [y[:, a : a + NB] for y in out3], [y[:, a:] for y in out3], TN
                        )

            else:
                m[o:t, :] = dot6(inverse, split3(c[o:t, order:]), NN)
            for lv, jj in ((0, 0), (0, 1), (0, 2), (0, 3), (1, 2), (1, 3), (2, 1)):
                if jj == j:

                    @pl.when(level == lv)
                    def _(lv=lv, jj=jj):
                        hook(lv, jj)

        for lv in range(3):

            @pl.when(level == lv)
            def _(lv=lv):
                after(lv)

        return carry

    lax.fori_loop(0, 3, one_level, 0)
    sends = [*nears, *g_gather, *g_shares, *across, *ex_g[1], *ex_g[2], ex_q[1], ex_q[2]]
    sends += [*sh_g[1], *sh_g[2], sh_q[1], sh_q[2], sh_s, *bag_shares]
    for copies in (*scatters, *gathers):
        sends += copies
    for copy in sends:
        copy.wait_send()


def mega(b3, b2, b1, rhs, leaf, cpl3, cpl2, cpl1):
    rows, r = b3.shape
    order = 2 * r
    chips = lax.axis_size("gy") // 2
    hr = r // 2
    pr = hr // chips
    most = max(len(y) for y in GROUPS)
    wide = pr * (most + 1)
    hbm = pl.BlockSpec(memory_space=pl.ANY)
    dma = pltpu.SemaphoreType.DMA

    def vmem(*shape):
        return pltpu.VMEM(shape, F32)

    return pl.pallas_call(
        lambda *refs: mega_kernel(chips, *refs),
        in_specs=[hbm] * 4 + [VMEM] + [hbm] * 3,
        out_specs=[VMEM] * 4,
        out_shape=[
            jax.ShapeDtypeStruct(shape, F32)
            for shape in ((3 * r, r), (16, order), (8, order), (4, order))
        ],
        scratch_shapes=[
            vmem(4, rows, r),
            pltpu.VMEM((3, r, rows), BF16),
            pltpu.VMEM((3, r, rows), BF16),
            vmem(4, most, r, r),
            vmem(4, most, hr, r),
            vmem(4, most, hr, r),
            vmem(4, chips - 1, most, pr, r),
            vmem(4, most, pr, r),
            vmem(4, most, pr, r),
            vmem(3, wide, r),
            vmem(3, 2, chips, wide, r),
            vmem(3, order, r),
            vmem(order, 3 * r),
            vmem(5, r, r),
            vmem(2, 1, r, r),
            vmem(order, 2 * r),
            vmem(r, 2 * r),
            vmem(hr, 2 * r),
            vmem(order, r),
            vmem(3, order, order),
            vmem(3, order, order),
            pltpu.VMEM((3, 3, order, order), BF16),
            pltpu.VMEM((3, 3, order, order), BF16),
            vmem(order, 2 * order),
            vmem(NB, NB),
            vmem(W, W // 8, 8, NB),
            vmem(order, order),
            vmem(order, 3 * r),
            vmem(r, 3 * r),
            vmem(r, 2 * r),
            vmem(NB, order),
            dma((7,)),
            dma((2, 4)),
            dma((2, 4, chips - 1)),
            dma((2, 2 * chips - 1)),
            dma((2, 2)),
            dma((2, 4)),
            dma((2, 3, chips - 1)),
            dma((2, 3)),
            dma((2, 3, 4)),
            dma((2, 3, 4)),
        ],
        compiler_params=pltpu.CompilerParams(
            collective_id=0, has_side_effects=True, vmem_limit_bytes=60 << 20
        ),
        name="mega",
    )(b3, b2, b1, rhs, leaf.reshape(rows // 128, 128), cpl3, cpl2, cpl1)


def apply_kernel(b3, b2, b1, rhs, leaf, x, k3, k2, k1, out, core3, core2, core1):
    r = b3.shape[1]

    @pl.when(pl.program_id(0) == 0)
    def _():
        core3[...] = k3[...]
        core2[...] = k2[...]
        core1[...] = k1[...]

    xs = split2(x[...])
    total = rhs[...]
    for i, b in enumerate((b3, b2, b1)):
        total = total - dot3(split2(b[...]), tuple(y[i * r : (i + 1) * r] for y in xs), NN)
    turned = leaf[0].T
    out[...] = total * jnp.concatenate([turned[:, u : u + 1] for u in range(leaf.shape[1])], 0)


def apply_update(b3, b2, b1, rhs, leaf, x, cores):
    rows, r = b3.shape
    tile = 512
    block = pl.BlockSpec((tile, r), lambda i: (i, 0))
    whole = [pl.BlockSpec(k.shape, lambda i: (0, 0)) for k in cores]
    return pl.pallas_call(
        apply_kernel,
        grid=(rows // tile,),
        in_specs=[block] * 4
        + [
            pl.BlockSpec((1, tile // 128, 128), lambda i: (i, 0, 0)),
            pl.BlockSpec(x.shape, lambda i: (0, 0)),
        ]
        + whole,
        out_specs=[block] + whole,
        out_shape=[jax.ShapeDtypeStruct(rhs.shape, F32)]
        + [jax.ShapeDtypeStruct(k.shape, F32) for k in cores],
        name="apply_update",
    )(b3, b2, b1, rhs, leaf.reshape(rows // tile, tile // 128, 128), x, *cores)


def per_device(basis3, basis2, basis1, leaf_inverse, rhs, coupling3, coupling2, coupling1):
    x, *cores = mega(
        basis3, basis2, basis1, rhs, leaf_inverse, coupling3, coupling2, coupling1
    )
    return tuple(apply_update(basis3, basis2, basis1, rhs, leaf_inverse, x, cores))


def solution(mesh):
    rows = P(("gx", "gy"), None)
    return jax.shard_map(
        per_device,
        mesh=mesh,
        in_specs=(rows, rows, rows, P(("gx", "gy")), rows, P(), P(), P()),
        out_specs=(rows, rows, rows, rows),
        check_vma=False,
    )
```
